32 devices in a mesh: space: 16 (over z, x, core), chan: 2 (over y).
Axes of the slice: x: 2, y: 2, z: 4, core: 2. Of those that a mesh axis runs over, the one named last changes fastest.
Arguments:
- features: bfloat16 [65536, 256], P('space'), may hold values from -6 to 6
- grad_out: bfloat16 [65536, 256], P('space', 'chan'), may hold values from -6 to 6
- weights: bfloat16 [27, 256, 256], P(None, None, 'chan'), may hold values from -0.078125 to 0.078125
- occupancy: int32 [65536], P('space'), may hold values 0 or 1
- block_list: int32 [16, 8], P('space'), may hold values from 0 to 7, each once within a row
- block_count: int32 [16], P('space'), may hold values from 1 to 8, as said below
Outputs:
- grad_features: bfloat16 [65536, 256], P('space', 'chan')
- grad_weights: float32 [6912, 256], P('space', 'chan')
The draws below stay inside these ranges and needn't reach their ends.
Inputs may be any that keep to these rules, and one draw needn't show every extreme that they name: `block_count`: some region has all 8 blocks active.
All inputs are finite; a program needn't handle non-finite values. No bound on the sum of `occupancy` on one device may be relied on, other than what follows from the above.
Results may differ from the reference program's by a relative error of at most 0.001.
Values may be sent and summed in bfloat16 or wider, within the bound.
No kernel may reach another device: no remote copies, remote signals or barrier semaphores. Data moves between devices by JAX's collectives and lax.ppermute only.
A program may use at most 64 MiB of HBM per device.

```python
import jax
import jax.numpy as jnp
from jax import lax

CIN = 256
COUT = 256
EDGE = 8
LAYERZ = 2
NBLK = 8
PSIDE = 2
PDEEP = 4
SITES = 65536
N_SPACE = 16


def draw_block_count(key, part):
    first_key, second_key = jax.random.split(jax.random.fold_in(key, 17))
    counts = jax.random.randint(first_key, (N_SPACE,), 1, NBLK + 1)
    chosen = jax.random.randint(second_key, (), 0, N_SPACE)
    return jnp.where(jnp.arange(N_SPACE) == chosen, NBLK, counts).astype(jnp.int32)


def set_ends(values, own_key, smallest, largest):
    longest = values.shape.index(max(values.shape))
    spots = []
    for shift in (0, 1):
        where = [jax.random.randint(jax.random.fold_in(own_key, axis), (), 0, length) for axis, length in enumerate(values.shape)]
        where[longest] = (where[longest] + shift) % values.shape[longest]
        spots.append(tuple(where))
    return values.at[spots[0]].set(smallest).at[spots[1]].set(largest)


def with_spikes(result, rng, source, target, shards_of, factor):
    def block_of(dim):
        return (jnp.arange(result.shape[dim]) // (result.shape[dim] // shards_of)).reshape((-1,) + (1,) * (result.ndim - 1 - dim))

    near = jax.random.permutation(rng, shards_of)[block_of(target)]
    second = (block_of(target) + shards_of // 2) % shards_of
    return jnp.where((block_of(source) == near) | (block_of(source) == second), factor * result, result)


def shard_levels(own_key, shape, cuts, least, top_value):
    factor_of, own = 1.0, jax.random.fold_in(own_key, 6)
    for dim, parts in cuts:
        heights = jnp.exp(jax.random.uniform(jax.random.fold_in(own, dim), (parts,), jnp.float32, least / len(cuts), top_value / len(cuts)))
        factor_of = factor_of * jnp.repeat(heights, shape[dim] // parts).reshape([-1 if axis == dim else 1 for axis in range(len(shape))])
    return factor_of


def normal_values(key, extent, deviation, bound, shards=(), held_as=jnp.bfloat16):
    gain = shard_levels(key, extent, shards, -0.22, 0.18) if shards else 1.0
    values = jax.random.normal(key, extent, jnp.float32) * deviation * gain
    return jnp.minimum(jnp.maximum(values, -bound), bound).astype(held_as)


def heavy_noise(key, dims, scale, most, cuts, heavy, kind=jnp.bfloat16):
    result = scale * jax.random.normal(key, dims, jnp.float32)
    if cuts:
        result = result * shard_levels(key, dims, cuts, -0.22, 0.18)
    return jnp.clip(with_spikes(result, jax.random.fold_in(key, 3), *heavy), -most, most).astype(kind)


def setup_inputs(seed: int = 0) -> dict:
    streams_of = jax.random.split(jax.random.key(seed), 7)
    return {
        "features": heavy_noise(streams_of[0], (SITES, CIN), 1.0, 6.0, ((0, 16),), (0, 1, 16, 2.0)),
        "grad_out": normal_values(streams_of[1], (SITES, COUT), 1.0, 6.0, ((0, 16), (1, 2))),
        "weights": normal_values(streams_of[2], (27, CIN, COUT), (27 * CIN) ** -0.5, 0.078125, ((2, 2),)),
        "occupancy": set_ends((jax.random.randint(streams_of[3], (SITES,), 0, 4) < 3).astype(jnp.int32), jax.random.fold_in(streams_of[3], 1), 0, 1),
        "block_list": jax.vmap(lambda own: jax.random.permutation(own, NBLK))(jax.random.split(streams_of[4], N_SPACE)).reshape((N_SPACE, NBLK)).astype(jnp.int32),
        "block_count": draw_block_count(jax.random.fold_in(streams_of[6], 71), 0),
    }


OFFSETS = [(first, second, third) for first in (-1, 0, 1) for second in (-1, 0, 1) for third in (-1, 0, 1)]

def reference(features, grad_out, weights, occupancy, block_list, block_count):
    span_xy = 2 * EDGE
    span_z = LAYERZ * EDGE
    block_slots = jnp.arange(NBLK, dtype=jnp.int32)
    position = lax.optimization_barrier(jnp.sum(jnp.where(block_list[:, :, None] == block_slots[None, None, :], block_slots[None, :, None], 0), axis=1))
    active_flag = (position < block_count[:, None]).astype(jnp.float32)
    block_grid = jnp.broadcast_to(active_flag.reshape(N_SPACE, 2, 1, 2, 1, LAYERZ, 1), (N_SPACE, 2, EDGE, 2, EDGE, LAYERZ, EDGE)).reshape(N_SPACE, span_xy, span_xy, span_z)
    cell_mask = block_grid * occupancy.reshape(N_SPACE, span_xy, span_xy, span_z).astype(jnp.float32)

    def spread(values, width):
        shaped = values.reshape(PSIDE, PSIDE, PDEEP, span_xy, span_xy, span_z, width)
        return shaped.transpose(0, 3, 1, 4, 2, 5, 6).reshape(PSIDE * span_xy, PSIDE * span_xy, PDEEP * span_z, width)
    map_mask = spread(cell_mask, 1)
    mask_bf = map_mask.astype(jnp.bfloat16)
    feat_masked = spread(features, CIN) * mask_bf
    grad_masked = spread(grad_out, COUT) * mask_bf
    size_x, size_y, size_z = (feat_masked.shape[0], feat_masked.shape[1], feat_masked.shape[2])
    pad_spec = ((1, 1), (1, 1), (1, 1), (0, 0))
    feat_pad = jnp.pad(feat_masked, pad_spec)
    grad_pad = jnp.pad(grad_masked, pad_spec)
    grad_flat = grad_masked.reshape(-1, COUT)
    data_grad = jnp.zeros((size_x * size_y * size_z, CIN), jnp.float32)
    weight_rows = []
    for tap_index, (off_x, off_y, off_z) in enumerate(OFFSETS):
        grad_slice = grad_pad[1 - off_x:1 - off_x + size_x, 1 - off_y:1 - off_y + size_y, 1 - off_z:1 - off_z + size_z].reshape(-1, COUT)
        data_grad = data_grad + jnp.dot(grad_slice, weights[tap_index].T, preferred_element_type=jnp.float32)
        feat_slice = feat_pad[1 + off_x:1 + off_x + size_x, 1 + off_y:1 + off_y + size_y, 1 + off_z:1 + off_z + size_z].reshape(-1, CIN)
        weight_rows.append(lax.dot_general(feat_slice, grad_flat, (((0,), (0,)), ((), ())), preferred_element_type=jnp.float32))
    data_grad = data_grad.reshape(size_x, size_y, size_z, CIN) * map_mask
    data_grad = data_grad.reshape(PSIDE, span_xy, PSIDE, span_xy, PDEEP, span_z, CIN).transpose(0, 2, 4, 1, 3, 5, 6).reshape(-1, CIN)
    grad_weights = jnp.concatenate(weight_rows, axis=0) * (1.0 / jnp.sqrt(jnp.float32(SITES)))
    return (data_grad.astype(jnp.bfloat16), grad_weights)
```

```python
import functools
import math

import jax
import jax.numpy as jnp
from jax import lax
from jax.experimental import pallas as pl
from jax.experimental.pallas import tpu as pltpu
from jax.sharding import PartitionSpec as P

EDGE = 8
LAYERZ = 2
NBLK = 8
SPAN = 2 * EDGE
PLANE = SPAN * SPAN
HALF = 128
BF = jnp.bfloat16
F32 = jnp.float32

SHIFTS = [(a, b) for a in (-1, 0, 1) for b in (-1, 0, 1)]
PAIRS = [(0, 1), (2, 3), (4, 5), (6, 7), (8,)]


def locate_side(device_total):
    plane_side = 1
    for candidate in range(1, 33):
        if 2 * candidate**3 == device_total:
            plane_side = candidate
    return plane_side


def prep_kernel(feat_ref, mask_ref, f_ref, fz_ref):
    lane = lax.broadcasted_iota(jnp.int32, (1, PLANE), 1) % SPAN
    keep_low = (lane != SPAN - 1).astype(F32)
    keep_high = (lane != 0).astype(F32)

    def plane(x, _):
        rows = pl.ds(pl.multiple_of(x * PLANE, PLANE), PLANE)
        block = feat_ref[rows, :].astype(F32).T * mask_ref[pl.ds(x, 1), :]
        cols = pl.ds(pl.multiple_of(x * PLANE, PLANE), PLANE)
        cin = block.shape[0]
        f_ref[0:cin, cols] = (pltpu.roll(block, 1, 1) * keep_high).astype(BF)
        f_ref[cin : 2 * cin, cols] = block.astype(BF)
        f_ref[2 * cin :, cols] = (pltpu.roll(block, PLANE - 1, 1) * keep_low).astype(BF)
        return 0

    lax.fori_loop(0, SPAN, plane, 0)


def prep(features, mask_rows):
    cells, cin = features.shape
    return pl.pallas_call(
        lambda a, m, f: prep_kernel(a, m, f, None),
        out_shape=jax.ShapeDtypeStruct((3 * cin, cells), BF),
        compiler_params=pltpu.CompilerParams(vmem_limit_bytes=56 << 20),
        cost_estimate=pl.CostEstimate(flops=0, bytes_accessed=cells * cin * 8, transcendentals=0),
        name="prep",
    )(features, mask_rows)


def weight_kernel(f_ref, fz_ref, gp_ref, zp_ref, out_ref, *, scale):
    cin = out_ref.shape[1]

    def source(shift):
        a, b = SHIFTS[shift]
        block = gp_ref[1 - a : 1 - a + SPAN, 1 - b : 1 - b + SPAN]
        return block.reshape(SPAN * PLANE, HALF)

    def face(side, shift):
        a, b = SHIFTS[shift]
        return zp_ref[side, b + 1, 1 - a : 1 - a + SPAN].reshape(PLANE, HALF)

    for pair in PAIRS:
        right = jnp.concatenate([source(s) for s in pair], axis=1)
        acc = jnp.dot(f_ref[...], right, preferred_element_type=F32)
        low = jnp.concatenate([face(0, s) for s in pair], axis=1)
        high = jnp.concatenate([face(1, s) for s in pair], axis=1)
        parts = [
            acc[0:cin] + jnp.dot(fz_ref[1], high, preferred_element_type=F32),
            acc[cin : 2 * cin],
            acc[2 * cin :] + jnp.dot(fz_ref[0], low, preferred_element_type=F32),
        ]
        for c in range(3):
            for k, s in enumerate(pair):
                out_ref[3 * s + c] = parts[c][:, HALF * k : HALF * (k + 1)] * scale


def weight_grad_local(f_all, fz, gp, zp, scale):
    cin = f_all.shape[0] // 3
    return pl.pallas_call(
        functools.partial(weight_kernel, scale=scale),
        out_shape=jax.ShapeDtypeStruct((27, cin, HALF), F32),
        compiler_params=pltpu.CompilerParams(vmem_limit_bytes=60 << 20),
        cost_estimate=pl.CostEstimate(
            flops=2 * 27 * cin * HALF * SPAN * PLANE, bytes_accessed=12 << 20, transcendentals=0
        ),
        name="weight_grad",
    )(f_all, fz, gp, zp)


def data_kernel(ga_ref, gb_ref, za_ref, zb_ref, wa_ref, wb_ref, mask_ref, out_ref, wt_ref, h_ref):
    for s in range(9):
        for half, ref in enumerate((wa_ref, wb_ref)):
            for c in range(3):
                tile = ref[3 * s + c].astype(F32).T.astype(BF)
                row = (2 * s + half) * HALF
                wt_ref[row : row + HALF, c * HALF : (c + 1) * HALF] = tile

    for side, c in ((0, 2), (1, 0)):
        cols = []
        for s in range(9):
            a, b = SHIFTS[s]
            for ref in (za_ref, zb_ref):
                cols.append(ref[side, b + 1, 1 - a : 1 - a + SPAN].reshape(PLANE, HALF))
        h_ref[side] = jnp.dot(
            jnp.concatenate(cols, axis=1),
            wt_ref[:, c * HALF : (c + 1) * HALF],
            preferred_element_type=F32,
        ).reshape(SPAN, SPAN, HALF)

    zpos = lax.broadcasted_iota(jnp.int32, (SPAN, SPAN, HALF), 1)

    def plane(x, _):
        cols = []
        for s in range(9):
            a, b = SHIFTS[s]
            for ref in (ga_ref, gb_ref):
                block = ref[pl.ds(x + 1 - a, 1), 1 - b : 1 - b + SPAN]
                cols.append(block.reshape(PLANE, HALF))
        prod = jnp.dot(
            jnp.concatenate(cols, axis=1), wt_ref[...], preferred_element_type=F32
        )
        down = pltpu.roll(prod[:, 0:HALF], PLANE - 1, 0).reshape(SPAN, SPAN, HALF)
        mid = prod[:, HALF : 2 * HALF].reshape(SPAN, SPAN, HALF)
        up = pltpu.roll(prod[:, 2 * HALF :], 1, 0).reshape(SPAN, SPAN, HALF)
        low = h_ref[0, pl.ds(x, 1)].reshape(SPAN, 1, HALF)
        high = h_ref[1, pl.ds(x, 1)].reshape(SPAN, 1, HALF)
        total = mid + jnp.where(zpos == 0, low, up) + jnp.where(zpos == SPAN - 1, high, down)
        keep = jnp.broadcast_to(mask_ref[pl.ds(x, 1), :], (8, PLANE)).T[:, 0:1]
        rows = pl.ds(pl.multiple_of(x * PLANE, PLANE), PLANE)
        out_ref[rows, :] = (total.reshape(PLANE, HALF) * keep).astype(BF)
        return 0

    lax.fori_loop(0, SPAN, plane, 0)


def data_grad_local(ga, gb, za, zb, wa, wb, mask_rows):
    return pl.pallas_call(
        data_kernel,
        out_shape=jax.ShapeDtypeStruct((SPAN * PLANE, HALF), BF),
        scratch_shapes=[
            pltpu.VMEM((18 * HALF, 3 * HALF), BF),
            pltpu.VMEM((2, SPAN, SPAN, HALF), F32),
        ],
        compiler_params=pltpu.CompilerParams(vmem_limit_bytes=56 << 20),
        cost_estimate=pl.CostEstimate(
            flops=2 * 27 * 2 * HALF * HALF * SPAN * PLANE, bytes_accessed=8 << 20, transcendentals=0
        ),
        name="data_grad",
    )(ga, gb, za, zb, wa, wb, mask_rows)


def extend(block, dim, stride, coords, side):
    total = lax.axis_size("space")
    length = block.shape[dim]
    first = lax.slice_in_dim(block, 0, 1, axis=dim)
    last = lax.slice_in_dim(block, length - 1, length, axis=dim)
    up = [(i, i + stride) for i in range(total) if coords(i) < side - 1]
    down = [(i + stride, i) for i, _ in [(j, 0) for j in range(total) if coords(j) < side - 1]]
    below = lax.ppermute(last, "space", up)
    above = lax.ppermute(first, "space", down)
    return jnp.concatenate([below, block, above], axis=dim)


def halo(grad, plane_side, depth):
    low = lax.slice_in_dim(grad, 0, 1, axis=2)
    block = extend(grad, 2, 1, lambda i: i % depth, depth)
    block = extend(block, 1, depth, lambda i: i // depth % plane_side, plane_side)
    block = extend(block, 0, depth * plane_side, lambda i: i // (depth * plane_side), plane_side)
    return block


def split_z(block):
    inner = block[:, :, 1 : 1 + SPAN]
    faces = jnp.stack([block[:, :, 0], block[:, :, SPAN + 1]])
    turned = jnp.stack([faces[:, :, 1 - b : 1 - b + SPAN] for b in (-1, 0, 1)], axis=1)
    return inner, turned


def swap_bit(block, bit, total):
    return lax.ppermute(block, "space", [(i, i ^ (1 << bit)) for i in range(total)])


def halve(block, axis, bit, index, total):
    mine = index // (1 << bit) % 2
    send = lax.dynamic_index_in_dim(block, 1 - mine, axis, keepdims=False)
    keep = lax.dynamic_index_in_dim(block, mine, axis, keepdims=False)
    return keep + swap_bit(send, bit, total)


def scatter_sum(partial, index, total):
    bits = total.bit_length() - 1
    rows = partial.shape[0] // total
    block = partial.reshape((2,) * bits + (rows, HALF))
    block = halve(block, bits - 1, 0, index, total)
    cut = rows // 2
    left = list(range(1, bits))
    first, second = block[..., :cut, :], block[..., cut:, :]
    have = sorted(left, reverse=True)
    for bit in left:
        first = halve(first, have.index(bit), bit, index, total)
        have.remove(bit)
    have = sorted(left, reverse=True)
    for bit in left[1:] + left[:1]:
        second = halve(second, have.index(bit), bit, index, total)
        have.remove(bit)
    return jnp.concatenate([first, second], axis=0)


def body(features, grad_out, weights, occupancy, block_list, block_count):
    total = lax.axis_size("space")
    plane_side = locate_side(total)
    depth = 2 * plane_side
    cells, cin = features.shape
    index = lax.axis_index("space")
    column = lax.axis_index("chan")

    block_order = block_list[0]
    live_count = block_count[0]
    slots = jnp.arange(NBLK, dtype=jnp.int32)
    position = jnp.sum(
        jnp.where(block_order[:, None] == slots[None, :], slots[:, None], 0), axis=0
    )
    active = (position < live_count).astype(F32)
    grid = jnp.broadcast_to(
        active.reshape(2, 1, 2, 1, LAYERZ, 1), (2, EDGE, 2, EDGE, LAYERZ, EDGE)
    ).reshape(SPAN, PLANE)
    mask_rows = grid * occupancy.reshape(SPAN, PLANE).astype(F32)
    grad = grad_out.reshape(SPAN, SPAN, SPAN, HALF) * mask_rows.astype(BF).reshape(
        SPAN, SPAN, SPAN, 1
    )

    theirs = lax.dynamic_slice_in_dim(weights, (1 - column) * HALF, HALF, axis=1)
    own_w = lax.dynamic_slice_in_dim(weights, column * HALF, HALF, axis=1)
    swap = [(0, 1), (1, 0)]
    other_w = lax.ppermute(theirs, "chan", swap)

    full = halo(grad, plane_side, depth)
    gp, zp = split_z(full)
    other = lax.ppermute(full, "chan", swap)
    ogp, ozp = split_z(other)

    f_all = prep(features, mask_rows)
    plain = f_all[cin : 2 * cin].reshape(cin, PLANE, SPAN)
    fz = jnp.stack([plain[:, :, 0], plain[:, :, SPAN - 1]])
    scale = 1.0 / math.sqrt(cells * total)
    partial = weight_grad_local(f_all, fz, gp, zp, scale).reshape(27 * cin, HALF)
    weight_out = scatter_sum(partial, index, total)

    data_out = data_grad_local(gp, ogp, zp, ozp, own_w, other_w, mask_rows)
    return data_out, weight_out


def solution(mesh):
    placed = (
        P("space", None),
        P("space", "chan"),
        P(None, None, "chan"),
        P("space"),
        P("space", None),
        P("space"),
    )
    return jax.shard_map(
        body,
        mesh=mesh,
        in_specs=placed,
        out_specs=(P("space", "chan"), P("space", "chan")),
        check_vma=False,
    )
```

```python
import functools
import math

import jax
import jax.numpy as jnp
from jax import lax
from jax.experimental import pallas as pl
from jax.experimental.pallas import tpu as pltpu
from jax.sharding import PartitionSpec as P

EDGE = 8
LAYERZ = 2
NBLK = 8
SPAN = 2 * EDGE
PLANE = SPAN * SPAN
HALF = 128
BF = jnp.bfloat16
F32 = jnp.float32

SHIFTS = [(a, b) for a in (-1, 0, 1) for b in (-1, 0, 1)]
PAIRS = [(0, 1), (2, 3), (4, 5), (6, 7), (8,)]


def locate_side(device_total):
    plane_side = 1
    for candidate in range(1, 33):
        if 2 * candidate**3 == device_total:
            plane_side = candidate
    return plane_side


def keep_column(mask_ref, x):
    return jnp.broadcast_to(mask_ref[x : x + 1, :], (8, PLANE)).T[:, 0:1]


def assemble(raw_ref, mask_ref, xb_ref, yb_ref, gp_ref):
    gp_ref[0] = xb_ref[0]
    gp_ref[SPAN + 1] = xb_ref[1]
    for x in range(SPAN):
        block = raw_ref[x * PLANE : (x + 1) * PLANE, :].astype(F32) * keep_column(mask_ref, x)
        gp_ref[x + 1, 1 : 1 + SPAN] = block.astype(BF).reshape(SPAN, SPAN, HALF)
        gp_ref[x + 1, 0] = yb_ref[0, x]
        gp_ref[x + 1, SPAN + 1] = yb_ref[1, x]


def prep_kernel(feat_ref, faces_ref, mask_ref, f_ref, fz_ref):
    lane = lax.broadcasted_iota(jnp.int32, (1, PLANE), 1) % SPAN
    keep_low = (lane != SPAN - 1).astype(F32)
    keep_high = (lane != 0).astype(F32)
    cin = fz_ref.shape[1]

    for x in range(SPAN):
        cols = slice(x * PLANE, (x + 1) * PLANE)
        block = feat_ref[cols, :].astype(F32).T * mask_ref[x : x + 1, :]
        f_ref[0:cin, cols] = (pltpu.roll(block, 1, 1) * keep_high).astype(BF)
        f_ref[cin : 2 * cin, cols] = block.astype(BF)
        f_ref[2 * cin :, cols] = (pltpu.roll(block, PLANE - 1, 1) * keep_low).astype(BF)
    for side in range(2):
        fz_ref[side] = faces_ref[side].astype(F32).T.astype(BF)


def prep(features, faces, mask_rows):
    cells, cin = features.shape
    return pl.pallas_call(
        prep_kernel,
        out_shape=(
            jax.ShapeDtypeStruct((3 * cin, cells), BF),
            jax.ShapeDtypeStruct((2, cin, PLANE), BF),
        ),
        compiler_params=pltpu.CompilerParams(vmem_limit_bytes=56 << 20),
        cost_estimate=pl.CostEstimate(flops=0, bytes_accessed=cells * cin * 8, transcendentals=0),
        name="prep",
    )(features, faces, mask_rows)


def weight_kernel(
    mine_ref, f_ref, fz_ref, raw_ref, mask_ref, xb_ref, yb_ref, zp_ref,
    keep_ref, send_ref, gp_ref, acc_ref, sems, *, scale
):
    assemble(raw_ref, mask_ref, xb_ref, yb_ref, gp_ref)
    cin = f_ref.shape[0] // 3
    rows = acc_ref.shape[2]

    def source(shift):
        a, b = SHIFTS[shift]
        block = gp_ref[1 - a : 1 - a + SPAN, 1 - b : 1 - b + SPAN]
        return block.reshape(SPAN * PLANE, HALF)

    def face(side, shift):
        a, b = SHIFTS[shift]
        return zp_ref[side, b + 1, 1 - a : 1 - a + SPAN].reshape(PLANE, HALF)

    def store(tap, value):
        first = tap * cin
        while first < (tap + 1) * cin:
            block, at = divmod(first, rows)
            count = min(rows - at, (tap + 1) * cin - first)
            piece = value[first - tap * cin : first - tap * cin + count]
            acc_ref[block % 2, block // 2, at : at + count] = piece
            first += count

    for pair in PAIRS:
        right = jnp.concatenate([source(s) for s in pair], axis=1)
        acc = jnp.dot(f_ref[...], right, preferred_element_type=F32)
        low = jnp.concatenate([face(0, s) for s in pair], axis=1)
        high = jnp.concatenate([face(1, s) for s in pair], axis=1)
        parts = [
            acc[0:cin] + jnp.dot(fz_ref[1], high, preferred_element_type=F32),
            acc[cin : 2 * cin],
            acc[2 * cin :] + jnp.dot(fz_ref[0], low, preferred_element_type=F32),
        ]
        for c in range(3):
            for k, s in enumerate(pair):
                store(3 * s + c, parts[c][:, HALF * k : HALF * (k + 1)] * scale)

    mine = mine_ref[0]
    out_send = pltpu.make_async_copy(acc_ref.at[1 - mine], send_ref, sems.at[0])
    out_keep = pltpu.make_async_copy(acc_ref.at[mine], keep_ref, sems.at[1])
    out_send.start()
    out_keep.start()
    out_send.wait()
    out_keep.wait()


VMEM_SPEC = pl.BlockSpec(memory_space=pltpu.VMEM)
SMEM_SPEC = pl.BlockSpec(memory_space=pltpu.SMEM)
ANY_SPEC = pl.BlockSpec(memory_space=pl.ANY)


def weight_grad_local(mine, f_all, fz, raw, mask_rows, borders, scale, total):
    cin = f_all.shape[0] // 3
    rows = 27 * cin // total
    out = jax.ShapeDtypeStruct((total // 2, rows, HALF), F32)
    return pl.pallas_call(
        functools.partial(weight_kernel, scale=scale),
        out_shape=(out, out),
        in_specs=[SMEM_SPEC] + [VMEM_SPEC] * 7,
        out_specs=(ANY_SPEC, ANY_SPEC),
        scratch_shapes=[
            pltpu.VMEM((SPAN + 2, SPAN + 2, SPAN, HALF), BF),
            pltpu.VMEM((2, total // 2, rows, HALF), F32),
            pltpu.SemaphoreType.DMA((2,)),
        ],
        compiler_params=pltpu.CompilerParams(vmem_limit_bytes=60 << 20),
        cost_estimate=pl.CostEstimate(
            flops=2 * 27 * cin * HALF * SPAN * PLANE, bytes_accessed=12 << 20, transcendentals=0
        ),
        name="weight_grad",
    )(mine, f_all, fz, raw, mask_rows, *borders)


def data_kernel(raw_ref, mask_ref, xb_ref, yb_ref, zp_ref, w_ref, *refs):
    if len(refs) == 5:
        prev_ref, out_ref, gp_ref, wt_ref, h_ref = refs
    else:
        (out_ref, gp_ref, wt_ref, h_ref), prev_ref = refs, None
    assemble(raw_ref, mask_ref, xb_ref, yb_ref, gp_ref)
    for s in range(9):
        for c in range(3):
            tile = w_ref[3 * s + c].astype(F32).T.astype(BF)
            wt_ref[s * HALF : (s + 1) * HALF, c * HALF : (c + 1) * HALF] = tile

    for side, c in ((0, 2), (1, 0)):
        cols = []
        for s in range(9):
            a, b = SHIFTS[s]
            cols.append(zp_ref[side, b + 1, 1 - a : 1 - a + SPAN].reshape(PLANE, HALF))
        h_ref[side] = jnp.dot(
            jnp.concatenate(cols, axis=1),
            wt_ref[:, c * HALF : (c + 1) * HALF],
            preferred_element_type=F32,
        ).reshape(SPAN, SPAN, HALF)

    zpos = lax.broadcasted_iota(jnp.int32, (SPAN, SPAN, HALF), 1)

    def plane(x, _):
        cols = []
        for s in range(9):
            a, b = SHIFTS[s]
            block = gp_ref[pl.ds(x + 1 - a, 1), 1 - b : 1 - b + SPAN]
            cols.append(block.reshape(PLANE, HALF))
        prod = jnp.dot(jnp.concatenate(cols, axis=1), wt_ref[...], preferred_element_type=F32)
        down = pltpu.roll(prod[:, 0:HALF], PLANE - 1, 0).reshape(SPAN, SPAN, HALF)
        mid = prod[:, HALF : 2 * HALF].reshape(SPAN, SPAN, HALF)
        up = pltpu.roll(prod[:, 2 * HALF :], 1, 0).reshape(SPAN, SPAN, HALF)
        low = h_ref[0, pl.ds(x, 1)].reshape(SPAN, 1, HALF)
        high = h_ref[1, pl.ds(x, 1)].reshape(SPAN, 1, HALF)
        full = mid + jnp.where(zpos == 0, low, up) + jnp.where(zpos == SPAN - 1, high, down)
        full = full.reshape(PLANE, HALF)
        rows = pl.ds(pl.multiple_of(x * PLANE, PLANE), PLANE)
        if prev_ref is None:
            out_ref[rows, :] = full
        else:
            keep = jnp.broadcast_to(mask_ref[pl.ds(x, 1), :], (8, PLANE)).T[:, 0:1]
            out_ref[rows, :] = ((full + prev_ref[rows, :]) * keep).astype(BF)
        return 0

    lax.fori_loop(0, SPAN, plane, 0, unroll=2)


def data_grad_local(raw, mask_rows, borders, tiles, before=None):
    args = (raw, mask_rows, *borders, tiles) + (() if before is None else (before,))
    return pl.pallas_call(
        data_kernel,
        out_shape=jax.ShapeDtypeStruct((SPAN * PLANE, HALF), F32 if before is None else BF),
        in_specs=[VMEM_SPEC] * len(args),
        out_specs=VMEM_SPEC,
        scratch_shapes=[
            pltpu.VMEM((SPAN + 2, SPAN + 2, SPAN, HALF), BF),
            pltpu.VMEM((9 * HALF, 3 * HALF), BF),
            pltpu.VMEM((2, SPAN, SPAN, HALF), F32),
        ],
        compiler_params=pltpu.CompilerParams(vmem_limit_bytes=56 << 20),
        cost_estimate=pl.CostEstimate(
            flops=2 * 27 * HALF * HALF * SPAN * PLANE, bytes_accessed=6 << 20, transcendentals=0
        ),
        name="data_grad",
    )(*args)


def split_kernel(bits_ref, keep_ref, recv_ref, *outs, bounds):
    for k, (low, high, lead) in enumerate(bounds):
        stay_ref, go_ref = outs[2 * k], outs[2 * k + 1]
        shape = keep_ref.shape
        mine = bits_ref[k]
        before = math.prod(shape[:lead])
        for ref, bit in ((stay_ref, mine), (go_ref, 1 - mine)):
            for i in range(before):
                at = []
                for size in reversed(shape[:lead]):
                    i, rest = divmod(i, size)
                    at.insert(0, rest)
                at = tuple(at)
                tail = (slice(None),) * (len(shape) - 3 - lead)
                src = at + (bit,) + tail + (slice(low, high),)
                ref[at] = keep_ref[src] + recv_ref[src]


def split(keep, recv, bits, bounds):
    outs = []
    for low, high, lead in bounds:
        shape = keep.shape[:lead] + keep.shape[lead + 1 : -2] + (high - low, HALF)
        outs += [jax.ShapeDtypeStruct(shape, F32)] * 2
    return pl.pallas_call(
        functools.partial(split_kernel, bounds=bounds),
        out_shape=tuple(outs),
        in_specs=[SMEM_SPEC, VMEM_SPEC, VMEM_SPEC],
        out_specs=tuple(VMEM_SPEC for _ in outs),
        compiler_params=pltpu.CompilerParams(vmem_limit_bytes=32 << 20),
        cost_estimate=pl.CostEstimate(
            flops=keep.size, bytes_accessed=16 * keep.size, transcendentals=0
        ),
        name="add_split",
    )(jnp.stack(bits), keep, recv)


def swap_bit(block, bit, total):
    return lax.ppermute(block, "space", [(i, i ^ (1 << bit)) for i in range(total)])


def bit_of(index, bit):
    return (index // (1 << bit) % 2).astype(jnp.int32)


def extend(block, dim, stride, coords, side):
    total = lax.axis_size("space")
    length = block.shape[dim]
    first = lax.slice_in_dim(block, 0, 1, axis=dim)
    last = lax.slice_in_dim(block, length - 1, length, axis=dim)
    below = lax.ppermute(
        last, "space", [(i, i + stride) for i in range(total) if coords(i) < side - 1]
    )
    above = lax.ppermute(
        first, "space", [(i + stride, i) for i in range(total) if coords(i) < side - 1]
    )
    return jnp.concatenate([below, block, above], axis=dim)


def turned(face):
    return jnp.stack([face[:, 1 - b : 1 - b + SPAN] for b in (-1, 0, 1)])


def wide_borders(masked, zl, zh, plane_side, depth):
    block = jnp.concatenate([zl[:, :, None], masked, zh[:, :, None]], axis=2)
    block = extend(block, 1, depth, lambda i: i // depth % plane_side, plane_side)
    block = extend(block, 0, depth * plane_side, lambda i: i // (depth * plane_side), plane_side)
    inner = block[:, :, 1 : 1 + SPAN]
    xb = jnp.stack([inner[0], inner[SPAN + 1]])
    yb = jnp.stack([inner[1 : 1 + SPAN, 0], inner[1 : 1 + SPAN, SPAN + 1]])
    zp = jnp.stack([turned(block[:, :, 0]), turned(block[:, :, SPAN + 1])])
    return xb, yb, zp


def pair_borders(cx, cy, xh, yh, eh, zl, zh):
    def both(value, coord, axis):
        zero = jnp.zeros_like(value)
        low = jnp.where(coord == 1, value, zero)
        high = jnp.where(coord == 0, value, zero)
        return jnp.expand_dims(low, axis), jnp.expand_dims(high, axis)

    def around(values, corner, axis):
        low, high = both(corner, cy, axis)
        return jnp.concatenate([low, values, high], axis=axis)

    xb = jnp.concatenate(both(around(xh[:SPAN], eh[:SPAN], 0), cx, 0))
    yb = jnp.concatenate(both(yh[:SPAN], cy, 0))

    def face(z, k):
        rows = around(z, yh[k], 1)
        low, high = both(around(xh[k], eh[k], 0), cx, 0)
        return turned(jnp.concatenate([low, rows, high], axis=0))

    zp = jnp.stack([face(zl, SPAN), face(zh, SPAN + 1)])
    return xb, yb, zp


def body(features, grad_out, weights, occupancy, block_list, block_count):
    total = lax.axis_size("space")
    plane_side = locate_side(total)
    depth = 2 * plane_side
    cells, cin = features.shape
    index = lax.axis_index("space")
    column = lax.axis_index("chan")
    swap = [(0, 1), (1, 0)]

    other_raw = lax.ppermute(grad_out, "chan", swap)

    block_order = block_list[0]
    live_count = block_count[0]
    slots = jnp.arange(NBLK, dtype=jnp.int32)
    position = jnp.sum(
        jnp.where(block_order[:, None] == slots[None, :], slots[:, None], 0), axis=0
    )
    active = (position < live_count).astype(F32)
    grid = jnp.broadcast_to(
        active.reshape(2, 1, 2, 1, LAYERZ, 1), (2, EDGE, 2, EDGE, LAYERZ, EDGE)
    ).reshape(SPAN, PLANE)
    mask_rows = grid * occupancy.reshape(SPAN, PLANE).astype(F32)
    mask = mask_rows.reshape(SPAN, SPAN, SPAN, 1).astype(BF)
    cube = grad_out.reshape(SPAN, SPAN, SPAN, HALF)

    even = index % 2 == 0
    low = cube[:, :, 0] * mask[:, :, 0]
    high = cube[:, :, SPAN - 1] * mask[:, :, SPAN - 1]
    inside = [i for i in range(total) if i % depth % 2 == 1 and i % depth < depth - 1]
    second = [(i, i + 1) for i in inside] + [(i + 1, i) for i in inside]
    from_a = swap_bit(jnp.where(even, high, low), 0, total)
    from_b = lax.ppermute(jnp.where(even, low, high), "space", second)
    zl = jnp.where(even, from_b, from_a)
    zh = jnp.where(even, from_a, from_b)

    if plane_side == 2:
        cx = index // (2 * depth)
        cy = index // depth % 2
        sx, sy = 2 * depth, depth

        def at(values, axis, coord):
            size = values.shape[axis]
            return jnp.where(
                coord == 0,
                lax.index_in_dim(values, size - 1, axis, keepdims=False),
                lax.index_in_dim(values, 0, axis, keepdims=False),
            )

        xf = at(cube, 0, cx) * at(mask, 0, cx)
        yf = at(cube, 1, cy) * at(mask, 1, cy)
        ef = at(at(cube, 0, cx), 0, cy) * at(at(mask, 0, cx), 0, cy)
        xs = jnp.concatenate([xf, at(zl, 0, cx)[None], at(zh, 0, cx)[None]])
        ys = jnp.concatenate([yf, at(zl, 1, cy)[None], at(zh, 1, cy)[None]])
        es = jnp.concatenate(
            [ef, at(at(zl, 0, cx), 0, cy)[None], at(at(zh, 0, cx), 0, cy)[None]]
        )
        xh = lax.ppermute(xs, "space", [(i, i ^ sx) for i in range(total)])
        yh = lax.ppermute(ys, "space", [(i, i ^ sy) for i in range(total)])
        eh = lax.ppermute(es, "space", [(i, i ^ sx ^ sy) for i in range(total)])
        borders = pair_borders(cx, cy, xh, yh, eh, zl, zh)
        flat = jnp.concatenate(
            [
                xh.reshape(-1, HALF),
                yh.reshape(-1, HALF),
                zl.reshape(-1, HALF),
                zh.reshape(-1, HALF),
                jnp.pad(eh, ((0, 14), (0, 0))),
            ]
        )
        flat = lax.ppermute(flat, "chan", swap)
        n = (SPAN + 2) * SPAN
        oxh = flat[:n].reshape(SPAN + 2, SPAN, HALF)
        oyh = flat[n : 2 * n].reshape(SPAN + 2, SPAN, HALF)
        ozl = flat[2 * n : 2 * n + PLANE].reshape(SPAN, SPAN, HALF)
        ozh = flat[2 * n + PLANE : 2 * n + 2 * PLANE].reshape(SPAN, SPAN, HALF)
        oeh = flat[2 * n + 2 * PLANE : 2 * n + 2 * PLANE + SPAN + 2]
        other_borders = pair_borders(cx, cy, oxh, oyh, oeh, ozl, ozh)
    else:
        borders = wide_borders(cube * mask, zl, zh, plane_side, depth)
        other_borders = tuple(lax.ppermute(v, "chan", swap) for v in borders)

    theirs = lax.dynamic_slice_in_dim(weights, (1 - column) * HALF, HALF, axis=1)
    own_w = lax.dynamic_slice_in_dim(weights, column * HALF, HALF, axis=1)
    flat_w = theirs.reshape(2, 27 * HALF // 2, HALF)
    core = bit_of(index, 0)
    part = lax.ppermute(
        lax.dynamic_index_in_dim(flat_w, core, 0, keepdims=False), "chan", swap
    )
    part_b = swap_bit(part, 0, total)
    other_w = jnp.concatenate(
        [jnp.where(core == 0, part, part_b), jnp.where(core == 0, part_b, part)]
    ).reshape(27, HALF, HALF)

    by_z = features.reshape(PLANE, SPAN, cin)
    z_mask = mask.reshape(PLANE, SPAN, 1)
    faces = jnp.stack([by_z[:, 0] * z_mask[:, 0], by_z[:, SPAN - 1] * z_mask[:, SPAN - 1]])
    f_all, fz = prep(features, faces, mask_rows)
    scale = 1.0 / math.sqrt(cells * total)
    keep, send = weight_grad_local(
        core[None], f_all, fz, grad_out, mask_rows, borders, scale, total
    )

    recv = swap_bit(send, 0, total)
    bits = total.bit_length() - 1
    rows = keep.shape[1]
    cut = rows // 2
    keep = keep.reshape((2,) * (bits - 1) + (rows, HALF))
    recv = recv.reshape(keep.shape)
    orders = [list(range(1, bits)), list(range(2, bits)) + [1]]
    have = [list(range(bits - 1, 0, -1)) for _ in orders]
    bounds = [
        (0, cut, have[0].index(orders[0][0])),
        (cut, rows, have[1].index(orders[1][0])),
    ]
    stay1, go1, stay2, go2 = split(
        keep, recv, [bit_of(index, order[0]) for order in orders], bounds
    )
    stays, gos = [stay1, stay2], [go1, go2]
    partial_out = None
    for step in range(bits - 1):
        got = [swap_bit(go, order[step], total) for go, order in zip(gos, orders)]
        if step == 0:
            raw, gos[0] = lax.optimization_barrier((grad_out, gos[0]))
            partial_out = data_grad_local(raw, mask_rows, borders, own_w)
            got, partial_out = lax.optimization_barrier((got, partial_out))
        if step == 1:
            data_out = data_grad_local(
                other_raw, mask_rows, other_borders, other_w, partial_out
            )
            got, data_out = lax.optimization_barrier((got, data_out))
        if step == bits - 2:
            weight_out = jnp.concatenate([s + g for s, g in zip(stays, got)], axis=0)
            break
        for k, order in enumerate(orders):
            have[k].remove(order[step])
            nxt = order[step + 1]
            stays[k], gos[k] = split(
                stays[k],
                got[k],
                [bit_of(index, nxt)],
                [(0, stays[k].shape[-2], have[k].index(nxt))],
            )
    return data_out, weight_out

def solution(mesh):
    placed = (
        P("space", None),
        P("space", "chan"),
        P(None, None, "chan"),
        P("space"),
        P("space", None),
        P("space"),
    )
    return jax.shard_map(
        body,
        mesh=mesh,
        in_specs=placed,
        out_specs=(P("space", "chan"), P("space", "chan")),
        check_vma=False,
    )
```

```python
import functools
import math

import jax
import jax.numpy as jnp
from jax import lax
from jax.experimental import pallas as pl
from jax.experimental.pallas import tpu as pltpu
from jax.sharding import PartitionSpec as P

EDGE = 8
LAYERZ = 2
NBLK = 8
SPAN = 2 * EDGE
PLANE = SPAN * SPAN
HALF = 128
BF = jnp.bfloat16
F32 = jnp.float32

SHIFTS = [(a, b) for a in (-1, 0, 1) for b in (-1, 0, 1)]
PAIRS = [(0, 1), (2, 3), (4, 5), (6, 7), (8,)]


def locate_side(device_total):
    plane_side = 1
    for candidate in range(1, 33):
        if 2 * candidate**3 == device_total:
            plane_side = candidate
    return plane_side


VMEM_SPEC = pl.BlockSpec(memory_space=pltpu.VMEM)
SMEM_SPEC = pl.BlockSpec(memory_space=pltpu.SMEM)
HBM_SPEC = pl.BlockSpec(memory_space=pltpu.HBM)
ANY_SPEC = pl.BlockSpec(memory_space=pl.ANY)
TAPS = 14
COST = pl.CostEstimate(flops=1, bytes_accessed=1, transcendentals=0)
MARK = jax.ShapeDtypeStruct((8, HALF), F32)


def faces_kernel(place_ref, list_ref, count_ref, raw_ref, occ_ref, mask_ref, sa_ref, sb_ref, xf_ref, yf_ref):
    even, px, py = place_ref[0], place_ref[1], place_ref[2]
    count = count_ref[0]
    x_at = lax.broadcasted_iota(jnp.int32, (SPAN, PLANE), 0)
    q_at = lax.broadcasted_iota(jnp.int32, (SPAN, PLANE), 1)
    y_at, z_at = q_at // SPAN, q_at % SPAN
    block = (x_at // EDGE) * (2 * LAYERZ) + (y_at // EDGE) * LAYERZ + z_at // EDGE
    active = jnp.zeros((SPAN, PLANE), F32)
    for j in range(NBLK):
        live = jnp.where(j < count, 1.0, 0.0).astype(F32)
        active += jnp.where(block == list_ref[0, j], live, 0.0)
    mask_ref[...] = active * occ_ref[...].astype(F32)

    za = jnp.where(even == 1, SPAN - 1, 0)
    row = lax.broadcasted_iota(jnp.int32, (3 * SPAN, PLANE), 0)
    col = lax.broadcasted_iota(jnp.int32, (3 * SPAN, PLANE), 1)
    kind, at = row // SPAN, row % SPAN
    depth = jnp.where(kind == 0, za, SPAN - 1 - za)
    target = jnp.where(kind == 2, py * SPAN + at, at * SPAN + depth)
    chosen = (col == target).astype(F32)
    for x in range(SPAN):
        left = (chosen * mask_ref[x : x + 1, :]).astype(BF)
        got = jnp.dot(left, raw_ref[x * PLANE : (x + 1) * PLANE, :], preferred_element_type=F32)
        got = got.astype(BF)
        sa_ref[x] = got[0:SPAN]
        sb_ref[x] = got[SPAN : 2 * SPAN]
        yf_ref[x] = got[2 * SPAN :]
    row = lax.broadcasted_iota(jnp.int32, (PLANE, PLANE), 0)
    col = lax.broadcasted_iota(jnp.int32, (PLANE, PLANE), 1)
    left = ((row == col).astype(F32) * mask_ref[pl.ds(px, 1), :]).astype(BF)
    plane = raw_ref[pl.ds(pl.multiple_of(px * PLANE, PLANE), PLANE), :]
    got = jnp.dot(left, plane, preferred_element_type=F32).astype(BF)
    xf_ref[...] = got.reshape(SPAN, SPAN, HALF)


def faces(place, block_list, block_count, raw, occupancy):
    face = jax.ShapeDtypeStruct((SPAN, SPAN, HALF), BF)
    return pl.pallas_call(
        faces_kernel,
        out_shape=(jax.ShapeDtypeStruct((SPAN, PLANE), F32), face, face, face, face),
        in_specs=[SMEM_SPEC] * 3 + [VMEM_SPEC] * 2,
        out_specs=(VMEM_SPEC,) * 5,
        compiler_params=pltpu.CompilerParams(vmem_limit_bytes=12 << 20),
        cost_estimate=COST,
        name="faces",
    )(place, block_list, block_count, raw, occupancy.reshape(SPAN, PLANE))


def edges_kernel(
    place_ref, fa_ref, fb_ref, xf_ref, yf_ref, w_ref, _, zl_ref, zh_ref, xs_ref, ys_ref, es_ref, part_ref, sem
):
    even, px, py = place_ref[0], place_ref[1], place_ref[2]
    copy = pltpu.make_async_copy(
        w_ref.at[pl.ds(place_ref[3], part_ref.shape[0]), pl.ds(pl.multiple_of(place_ref[4], HALF), HALF)],
        part_ref,
        sem,
    )
    copy.start()

    @pl.when(even == 1)
    def _():
        zl_ref[...] = fb_ref[...]
        zh_ref[...] = fa_ref[...]

    @pl.when(even == 0)
    def _():
        zl_ref[...] = fa_ref[...]
        zh_ref[...] = fb_ref[...]

    xs_ref[0:SPAN] = xf_ref[...]
    ys_ref[0:SPAN] = yf_ref[...]
    es_ref[0:SPAN, :] = yf_ref[pl.ds(px, 1)].reshape(SPAN, HALF)
    row = lax.broadcasted_iota(jnp.int32, (2 * SPAN, PLANE), 0)
    col = lax.broadcasted_iota(jnp.int32, (2 * SPAN, PLANE), 1)
    total = None
    for k, ref in enumerate((zl_ref, zh_ref)):
        xs_ref[SPAN + k] = ref[pl.ds(px, 1)].reshape(SPAN, HALF)
        target = jnp.where(
            row < SPAN, row * SPAN + py, jnp.where(row == SPAN + k, px * SPAN + py, -1)
        )
        left = (col == target).astype(F32).astype(BF)
        got = jnp.dot(left, ref[...].reshape(PLANE, HALF), preferred_element_type=F32)
        ys_ref[SPAN + k] = got[0:SPAN].astype(BF)
        total = got[SPAN:] if total is None else total + got[SPAN:]
    es_ref[SPAN:, :] = total.astype(BF)
    copy.wait()


def edges(place, from_a, from_b, xf, yf, weights, mark):
    face = jax.ShapeDtypeStruct((SPAN, SPAN, HALF), BF)
    strip = jax.ShapeDtypeStruct((SPAN + 2, SPAN, HALF), BF)
    corner = jax.ShapeDtypeStruct((2 * SPAN, HALF), BF)
    return pl.pallas_call(
        edges_kernel,
        out_shape=(
            face, face, strip, strip, corner,
            jax.ShapeDtypeStruct((TAPS, HALF, HALF), BF),
        ),
        in_specs=[SMEM_SPEC] + [VMEM_SPEC] * 4 + [HBM_SPEC, ANY_SPEC],
        out_specs=(VMEM_SPEC,) * 5 + (HBM_SPEC,),
        scratch_shapes=[pltpu.SemaphoreType.DMA],
        compiler_params=pltpu.CompilerParams(vmem_limit_bytes=8 << 20),
        cost_estimate=COST,
        name="edges",
    )(place, from_a, from_b, xf, yf, weights, mark)

def keep_column(mask_ref, x):
    return jnp.broadcast_to(mask_ref[x : x + 1, :], (8, PLANE)).T[:, 0:1]


def unpack(place_ref, flat_ref, gp_ref, zp_ref):
    cx, cy = place_ref[6], place_ref[7]
    near_x, far_x = (SPAN + 1) * (1 - cx), (SPAN + 1) * cx
    near_y, far_y = (SPAN + 1) * (1 - cy), (SPAN + 1) * cy
    n = (SPAN + 2) * SPAN
    zero = jnp.zeros((SPAN, HALF), BF)

    def rows(first, count=SPAN):
        return flat_ref[first : first + count, :]

    for x in range(SPAN + 2):
        gp_ref[far_x, x] = zero
        gp_ref[x, far_y] = zero
    for y in range(SPAN):
        gp_ref[near_x, y + 1] = rows(y * SPAN)
        gp_ref[y + 1, near_y] = rows(n + y * SPAN)
    gp_ref[near_x, far_y] = zero
    gp_ref[near_x, near_y] = rows(2 * n + 2 * PLANE)
    place = lax.broadcasted_iota(jnp.int32, (SPAN, SPAN, HALF), 1)
    single = lax.broadcasted_iota(jnp.int32, (SPAN, HALF), 0)
    for side in range(2):
        face = rows(2 * n + side * PLANE, PLANE).astype(F32).reshape(SPAN, SPAN, HALF)
        strip = rows(n + (SPAN + side) * SPAN).astype(F32)
        x_row = rows((SPAN + side) * SPAN).astype(F32)
        corner = flat_ref[2 * n + 2 * PLANE + SPAN :, :].astype(F32)[side : side + 1, :]
        low, high = (jnp.where(cy == want, strip, 0.0).reshape(SPAN, 1, HALF) for want in (1, 0))
        c_low, c_high = (jnp.where(cy == want, corner, 0.0) for want in (1, 0))
        moved = [
            jnp.where(place == SPAN - 1, high, jnp.roll(face, -1, 1)),
            face,
            jnp.where(place == 0, low, jnp.roll(face, 1, 1)),
        ]
        moved_row = [
            jnp.where(single == SPAN - 1, c_high, jnp.roll(x_row, -1, 0)),
            x_row,
            jnp.where(single == 0, c_low, jnp.roll(x_row, 1, 0)),
        ]
        for b in range(3):
            zp_ref[side, b, 1 : 1 + SPAN] = moved[b].astype(BF)
            zp_ref[side, b, far_x] = zero
            zp_ref[side, b, near_x] = moved_row[b].astype(BF)


def assemble(raw_refs, mask_ref, yb_ref, gp_ref):
    each = SPAN // len(raw_refs)
    for x in range(SPAN):
        rows = slice(x % each * PLANE, (x % each + 1) * PLANE)
        block = raw_refs[x // each][rows, :].astype(F32) * keep_column(mask_ref, x)
        gp_ref[x + 1, 1 : 1 + SPAN] = block.astype(BF).reshape(SPAN, SPAN, HALF)
        if yb_ref is not None:
            gp_ref[x + 1, 0] = yb_ref[0, x]
            gp_ref[x + 1, SPAN + 1] = yb_ref[1, x]


def load_features(feat_ref, mask_ref, f_ref, rims):
    cin = feat_ref.shape[1]
    src = lax.broadcasted_iota(jnp.int32, (PLANE, 3 * PLANE), 0)
    col = lax.broadcasted_iota(jnp.int32, (PLANE, 3 * PLANE), 1)
    dst = col % PLANE
    at = dst % SPAN + col // PLANE - 1
    shift = (at >= 0) & (at < SPAN) & (src == dst // SPAN * SPAN + at)
    shift = shift.astype(F32).astype(BF)

    def spread(block, *outs):
        moved = jnp.dot(block, shift, preferred_element_type=F32).astype(BF)
        for ref, cols in outs:
            ref[0:cin, cols] = moved[:, 0:PLANE]
            ref[cin : 2 * cin, cols] = block
            ref[2 * cin :, cols] = moved[:, 2 * PLANE :]

    row = lax.broadcasted_iota(jnp.int32, (4 * SPAN, PLANE), 0)
    pos = lax.broadcasted_iota(jnp.int32, (4 * SPAN, PLANE), 1)
    kind, r = row // SPAN, row % SPAN
    target = jnp.where(kind < 2, kind * (PLANE - SPAN) + r, r * SPAN + (kind - 2) * (SPAN - 1))
    chosen = (pos == target).astype(F32)
    found = []
    whole = slice(0, PLANE)
    for x in range(SPAN):
        cols = slice(x * PLANE, (x + 1) * PLANE)
        plane = feat_ref[cols, :]
        mask = mask_ref[x : x + 1, :]
        outs = [(f_ref, cols)]
        if rims and x in (0, SPAN - 1):
            outs.append((rims[0].at[x % 2], whole))
        spread((plane.T.astype(F32) * mask).astype(BF), *outs)
        if rims:
            left = (chosen * mask).astype(BF)
            found.append(jnp.dot(left, plane, preferred_element_type=F32))
    if rims:
        for side in range(2):
            rim = [v[side * SPAN : (side + 1) * SPAN] for v in found]
            spread(jnp.concatenate(rim, axis=0).astype(BF).T, (rims[1].at[side], whole))
            rim = [v[(side + 2) * SPAN : (side + 3) * SPAN] for v in found]
            rims[2][side] = jnp.concatenate(rim, axis=0).astype(BF).T


def inner_kernel(feat_ref, raw_ref, mask_ref, *refs, pairs, ignored):
    out_ref, mark_ref, *rims, f_ref, gp_ref, hold_ref, sems = refs[ignored:]
    cin = feat_ref.shape[1]
    copies = []

    def leave(source, target):
        copy = pltpu.make_async_copy(source, target, sems.at[len(copies)])
        copy.start()
        copies.append(copy)

    if rims:
        held = rims[3:]
        load_features(feat_ref, mask_ref, f_ref, held)
    else:
        load_features(feat_ref, mask_ref, f_ref, ())
    zero = jnp.zeros((SPAN, HALF), BF)
    for y in range(SPAN + 2):
        gp_ref[0, y] = zero
        gp_ref[SPAN + 1, y] = zero
    for x in range(SPAN):
        block = raw_ref[x * PLANE : (x + 1) * PLANE, :].astype(F32) * keep_column(mask_ref, x)
        gp_ref[x + 1, 1 : 1 + SPAN] = block.astype(BF).reshape(SPAN, SPAN, HALF)
        gp_ref[x + 1, 0] = zero
        gp_ref[x + 1, SPAN + 1] = zero

    def source(shift):
        a, b = SHIFTS[shift]
        block = gp_ref[1 - a : 1 - a + SPAN, 1 - b : 1 - b + SPAN]
        return block.reshape(SPAN * PLANE, HALF)

    mark_ref[...] = jnp.zeros_like(mark_ref)
    for pair in pairs:
        right = jnp.concatenate([source(s) for s in pair], axis=1)
        acc = jnp.dot(f_ref[...], right, preferred_element_type=F32)
        for c in range(3):
            for k, s in enumerate(pair):
                tap = 3 * (s - pairs[0][0]) + c
                hold_ref[tap] = acc[c * cin : (c + 1) * cin, HALF * k : HALF * (k + 1)]
    leave(hold_ref, out_ref)
    if rims:
        for source, target in zip(held, rims[:3]):
            leave(source, target)
    for copy in copies:
        copy.wait()


def weight_grad_inner(features, raw, mask_rows, pairs, with_rims, *ahead):
    cells, cin = features.shape
    taps = 3 * sum(len(pair) for pair in pairs)
    outs = [jax.ShapeDtypeStruct((taps, cin, HALF), F32), MARK]
    held = []
    if with_rims:
        held = [(2, 3 * cin, PLANE), (2, 3 * cin, PLANE), (2, cin, PLANE)]
        outs += [jax.ShapeDtypeStruct(shape, BF) for shape in held]
    return pl.pallas_call(
        functools.partial(inner_kernel, pairs=pairs, ignored=len(ahead)),
        out_shape=tuple(outs),
        in_specs=[VMEM_SPEC] * 3 + [ANY_SPEC] * len(ahead),
        out_specs=(HBM_SPEC, VMEM_SPEC) + (HBM_SPEC,) * len(held),
        scratch_shapes=[pltpu.VMEM(shape, BF) for shape in held]
        + [
            pltpu.VMEM((3 * cin, cells), BF),
            pltpu.VMEM((SPAN + 2, SPAN + 2, SPAN, HALF), BF),
            pltpu.VMEM((taps, cin, HALF), F32),
            pltpu.SemaphoreType.DMA((len(held) + 1,)),
        ],
        compiler_params=pltpu.CompilerParams(vmem_limit_bytes=28 << 20),
        cost_estimate=COST,
        name="weight_inner",
    )(features, raw, mask_rows, *ahead)


def rim_kernel(
    mine_ref, fx_ref, fy_ref, fz_ref, xb_ref, yb_ref, zp_ref, part_a_ref, part_b_ref,
    *refs, scale, pieces, ignored
):
    parts, refs = refs[:pieces], refs[pieces + ignored :]
    keep_ref, send_ref, *flat_refs, acc_ref, sems = refs
    at = 0
    for ref in parts:
        for block in range(ref.shape[0] if len(ref.shape) == 3 else 1):
            value = ref[block] if len(ref.shape) == 3 else ref[...]
            flat_refs[0][at : at + value.shape[0], :] = value
            at += value.shape[0]
    cin = fz_ref.shape[1]
    rows = acc_ref.shape[2]
    zero = jnp.zeros((1, SPAN, HALF), BF)
    more = {}

    def add(shift, c, value):
        more.setdefault(3 * shift + c, []).append(value)

    for side in range(2):
        first = 6 if side == 0 else 0
        right = jnp.concatenate(
            [xb_ref[side, 1 - b : 1 - b + SPAN].reshape(PLANE, HALF) for b in (-1, 0, 1)], axis=1
        )
        got = jnp.dot(fx_ref[side], right, preferred_element_type=F32)
        for b in range(3):
            for c in range(3):
                add(first + b, c, got[c * cin : (c + 1) * cin, b * HALF : (b + 1) * HALF])
        strip = jnp.concatenate([zero, yb_ref[side], zero], axis=0)
        right = jnp.concatenate(
            [strip[1 - a : 1 - a + SPAN].reshape(PLANE, HALF) for a in (-1, 0, 1)], axis=1
        )
        got = jnp.dot(fy_ref[side], right, preferred_element_type=F32)
        for a in range(3):
            for c in range(3):
                shift = 3 * a + (2 if side == 0 else 0)
                add(shift, c, got[c * cin : (c + 1) * cin, a * HALF : (a + 1) * HALF])
        for pair in PAIRS:
            cols = []
            for s in pair:
                a, b = SHIFTS[s]
                cols.append(zp_ref[side, b + 1, 1 - a : 1 - a + SPAN].reshape(PLANE, HALF))
            got = jnp.dot(
                fz_ref[side], jnp.concatenate(cols, axis=1), preferred_element_type=F32
            )
            for k, s in enumerate(pair):
                add(s, 2 if side == 0 else 0, got[:, k * HALF : (k + 1) * HALF])

    for tap in range(27):
        taps_a = part_a_ref.shape[0]
        value = part_a_ref[tap] if tap < taps_a else part_b_ref[tap - taps_a]
        for extra in more.get(tap, []):
            value = value + extra
        value = value * scale
        first = tap * cin
        while first < (tap + 1) * cin:
            block, at = divmod(first, rows)
            count = min(rows - at, (tap + 1) * cin - first)
            piece = value[first - tap * cin : first - tap * cin + count]
            acc_ref[block % 2, block // 2, at : at + count] = piece
            first += count

    mine = mine_ref[0]
    out_send = pltpu.make_async_copy(acc_ref.at[1 - mine], send_ref, sems.at[0])
    out_keep = pltpu.make_async_copy(acc_ref.at[mine], keep_ref, sems.at[1])
    out_send.start()
    out_keep.start()
    out_send.wait()
    out_keep.wait()


def weight_grad_rim(mine, fx, fy, fz, borders, inner_a, inner_b, scale, total, pieces, *ahead):
    cin = fz.shape[1]
    rows = 27 * cin // total
    outs = [jax.ShapeDtypeStruct((total // 2, rows, HALF), F32)] * 2
    if pieces:
        length = sum(v.size for v in pieces) // HALF
        outs.append(jax.ShapeDtypeStruct((length, HALF), BF))
    return pl.pallas_call(
        functools.partial(rim_kernel, scale=scale, pieces=len(pieces), ignored=len(ahead)),
        out_shape=tuple(outs),
        in_specs=[SMEM_SPEC] + [VMEM_SPEC] * (8 + len(pieces)) + [ANY_SPEC] * len(ahead),
        out_specs=(ANY_SPEC, ANY_SPEC) + (VMEM_SPEC,) * (len(outs) - 2),
        scratch_shapes=[
            pltpu.VMEM((2, total // 2, rows, HALF), F32),
            pltpu.SemaphoreType.DMA((2,)),
        ],
        compiler_params=pltpu.CompilerParams(vmem_limit_bytes=24 << 20),
        cost_estimate=COST,
        name="weight_rim",
    )(mine, fx, fy, fz, *borders, inner_a, inner_b, *pieces, *ahead)


def data_kernel(place_ref, mask_ref, *refs, borders, ignored, last):
    around, refs = refs[:borders], refs[borders:]
    *refs, z_ref = refs
    if last:
        *raw_refs, wa_ref, wb_ref, prev_ref = refs[:5]
        out_ref, mark_ref, gp_ref, wt_ref, h_ref = refs[5 + ignored :]
        first_core = place_ref[0] == 1

        def tile_of(tap):
            low = min(tap, TAPS - 1)
            high = max(tap - (27 - TAPS), 0)
            if tap < 27 - TAPS:
                return jnp.where(first_core, wa_ref[low], wb_ref[low])
            if tap >= TAPS:
                return jnp.where(first_core, wb_ref[high], wa_ref[high])
            return jnp.where(first_core, wa_ref[low], wa_ref[high])
    else:
        raw_ref, whole_ref = refs[:2]
        out_ref, mark_ref, gp_ref, wt_ref, h_ref, w_ref, sem = refs[2 + ignored :]
        raw_refs, prev_ref = [raw_ref], None
        copy = pltpu.make_async_copy(whole_ref.at[:, pl.ds(pl.multiple_of(place_ref[5], HALF), HALF)], w_ref, sem)
        copy.start()

        def tile_of(tap):
            return w_ref[tap]

    mark_ref[...] = jnp.zeros_like(mark_ref)
    if borders == 1:
        zp_ref = z_ref
        unpack(place_ref, around[0], gp_ref, zp_ref)
        assemble(raw_refs, mask_ref, None, gp_ref)
    else:
        xb_ref, yb_ref, zp_ref = around
        gp_ref[0] = xb_ref[0]
        gp_ref[SPAN + 1] = xb_ref[1]
        assemble(raw_refs, mask_ref, yb_ref, gp_ref)
    if not last:
        copy.wait()
    for s in range(9):
        for c in range(3):
            tile = tile_of(3 * s + c).astype(F32).T.astype(BF)
            wt_ref[s * HALF : (s + 1) * HALF, c * HALF : (c + 1) * HALF] = tile

    for side, c in ((0, 2), (1, 0)):
        cols = []
        for s in range(9):
            a, b = SHIFTS[s]
            cols.append(zp_ref[side, b + 1, 1 - a : 1 - a + SPAN].reshape(PLANE, HALF))
        h_ref[side] = jnp.dot(
            jnp.concatenate(cols, axis=1),
            wt_ref[:, c * HALF : (c + 1) * HALF],
            preferred_element_type=F32,
        ).reshape(SPAN, SPAN, HALF)

    zpos = lax.broadcasted_iota(jnp.int32, (SPAN, SPAN, HALF), 1)

    def plane(x, _):
        cols = []
        for s in range(9):
            a, b = SHIFTS[s]
            block = gp_ref[pl.ds(x + 1 - a, 1), 1 - b : 1 - b + SPAN]
            cols.append(block.reshape(PLANE, HALF))
        prod = jnp.dot(jnp.concatenate(cols, axis=1), wt_ref[...], preferred_element_type=F32)
        down = pltpu.roll(prod[:, 0:HALF], PLANE - 1, 0).reshape(SPAN, SPAN, HALF)
        mid = prod[:, HALF : 2 * HALF].reshape(SPAN, SPAN, HALF)
        up = pltpu.roll(prod[:, 2 * HALF :], 1, 0).reshape(SPAN, SPAN, HALF)
        low = h_ref[0, pl.ds(x, 1)].reshape(SPAN, 1, HALF)
        high = h_ref[1, pl.ds(x, 1)].reshape(SPAN, 1, HALF)
        full = mid + jnp.where(zpos == 0, low, up) + jnp.where(zpos == SPAN - 1, high, down)
        full = full.reshape(PLANE, HALF)
        rows = pl.ds(pl.multiple_of(x * PLANE, PLANE), PLANE)
        if prev_ref is None:
            out_ref[rows, :] = full
        else:
            keep = jnp.broadcast_to(mask_ref[pl.ds(x, 1), :], (8, PLANE)).T[:, 0:1]
            out_ref[rows, :] = ((full + prev_ref[rows, :]) * keep).astype(BF)
        return 0

    lax.fori_loop(0, SPAN, plane, 0, unroll=4)


def data_grad_local(place, mask_rows, borders, operands, last, *ahead):
    scratch = [
        pltpu.VMEM((SPAN + 2, SPAN + 2, SPAN, HALF), BF),
        pltpu.VMEM((9 * HALF, 3 * HALF), BF),
        pltpu.VMEM((2, SPAN, SPAN, HALF), F32),
    ]
    specs = [VMEM_SPEC] * len(operands)
    if not last:
        specs[-1] = HBM_SPEC
        scratch += [pltpu.VMEM((27, HALF, HALF), BF), pltpu.SemaphoreType.DMA]
    scratch.append(pltpu.VMEM((2, 3, SPAN + 2, SPAN, HALF), BF))
    return pl.pallas_call(
        functools.partial(
            data_kernel, borders=len(borders), ignored=len(ahead), last=last
        ),
        out_shape=(
            jax.ShapeDtypeStruct((SPAN * PLANE, HALF), BF if last else F32),
            MARK,
        ),
        in_specs=[SMEM_SPEC] + [VMEM_SPEC] * (1 + len(borders)) + specs + [ANY_SPEC] * len(ahead),
        out_specs=(VMEM_SPEC, VMEM_SPEC),
        scratch_shapes=scratch,
        compiler_params=pltpu.CompilerParams(vmem_limit_bytes=20 << 20),
        cost_estimate=COST,
        name="data_grad",
    )(place, mask_rows, *borders, *operands, *ahead)


def split_kernel(bits_ref, keep_ref, recv_ref, *outs, bounds, ignored):
    outs = outs[ignored:]
    for k, (low, high, lead) in enumerate(bounds):
        stay_ref, go_ref = outs[2 * k], outs[2 * k + 1]
        shape = keep_ref.shape
        mine = bits_ref[k]
        before = math.prod(shape[:lead])
        for ref, bit in ((stay_ref, mine), (go_ref, 1 - mine)):
            for i in range(before):
                at = []
                for size in reversed(shape[:lead]):
                    i, rest = divmod(i, size)
                    at.insert(0, rest)
                at = tuple(at)
                tail = (slice(None),) * (len(shape) - 3 - lead)
                src = at + (bit,) + tail + (slice(low, high),)
                ref[at] = keep_ref[src] + recv_ref[src]


def split(keep, recv, bits, bounds, *ahead):
    outs = []
    for low, high, lead in bounds:
        shape = keep.shape[:lead] + keep.shape[lead + 1 : -2] + (high - low, HALF)
        outs += [jax.ShapeDtypeStruct(shape, F32)] * 2
    return pl.pallas_call(
        functools.partial(split_kernel, bounds=bounds, ignored=len(ahead)),
        out_shape=tuple(outs),
        in_specs=[SMEM_SPEC, VMEM_SPEC, VMEM_SPEC] + [ANY_SPEC] * len(ahead),
        out_specs=tuple(VMEM_SPEC for _ in outs),
        compiler_params=pltpu.CompilerParams(vmem_limit_bytes=12 << 20),
        cost_estimate=COST,
        name="add_split",
    )(jnp.stack(bits), keep, recv, *ahead)


def swap_bit(block, bit, total):
    return lax.ppermute(block, "space", [(i, i ^ (1 << bit)) for i in range(total)])


def bit_of(index, bit):
    return (index // (1 << bit) % 2).astype(jnp.int32)


def extend(block, dim, stride, coords, side):
    total = lax.axis_size("space")
    length = block.shape[dim]
    first = lax.slice_in_dim(block, 0, 1, axis=dim)
    last = lax.slice_in_dim(block, length - 1, length, axis=dim)
    below = lax.ppermute(
        last, "space", [(i, i + stride) for i in range(total) if coords(i) < side - 1]
    )
    above = lax.ppermute(
        first, "space", [(i + stride, i) for i in range(total) if coords(i) < side - 1]
    )
    return jnp.concatenate([below, block, above], axis=dim)


def turned(face):
    return jnp.stack([face[:, 1 - b : 1 - b + SPAN] for b in (-1, 0, 1)])


def wide_borders(masked, zl, zh, plane_side, depth):
    block = jnp.concatenate([zl[:, :, None], masked, zh[:, :, None]], axis=2)
    block = extend(block, 1, depth, lambda i: i // depth % plane_side, plane_side)
    block = extend(block, 0, depth * plane_side, lambda i: i // (depth * plane_side), plane_side)
    inner = block[:, :, 1 : 1 + SPAN]
    xb = jnp.stack([inner[0], inner[SPAN + 1]])
    yb = jnp.stack([inner[1 : 1 + SPAN, 0], inner[1 : 1 + SPAN, SPAN + 1]])
    zp = jnp.stack([turned(block[:, :, 0]), turned(block[:, :, SPAN + 1])])
    return xb, yb, zp


def pair_borders(cx, cy, xh, yh, eh, zl, zh):
    def both(value, coord, axis):
        zero = jnp.zeros_like(value)
        low = jnp.where(coord == 1, value, zero)
        high = jnp.where(coord == 0, value, zero)
        return jnp.expand_dims(low, axis), jnp.expand_dims(high, axis)

    def around(values, corner, axis):
        low, high = both(corner, cy, axis)
        return jnp.concatenate([low, values, high], axis=axis)

    xb = jnp.concatenate(both(around(xh[:SPAN], eh[:SPAN], 0), cx, 0))
    yb = jnp.concatenate(both(yh[:SPAN], cy, 0))

    def face(z, k):
        rows = around(z, yh[k], 1)
        low, high = both(around(xh[k], eh[k], 0), cx, 0)
        return turned(jnp.concatenate([low, rows, high], axis=0))

    zp = jnp.stack([face(zl, SPAN), face(zh, SPAN + 1)])
    return xb, yb, zp


def body(features, grad_out, weights, occupancy, block_list, block_count):
    total = lax.axis_size("space")
    plane_side = locate_side(total)
    depth = 2 * plane_side
    cells, cin = features.shape
    index = lax.axis_index("space")
    column = lax.axis_index("chan")
    swap = [(0, 1), (1, 0)]
    cx = index // (plane_side * depth)
    cy = index // depth % plane_side
    even = index % 2 == 0

    core = bit_of(index, 0)
    place = jnp.stack(
        [
            (index + 1) % 2,
            jnp.where(cx == 0, SPAN - 1, 0),
            jnp.where(cy == 0, SPAN - 1, 0),
            core * (27 - TAPS),
            (1 - column) * HALF,
            column * HALF,
            cx,
            cy,
        ]
    ).astype(jnp.int32)
    mask_rows, send_a, send_b, xf, yf = faces(
        place, block_list, block_count, grad_out, occupancy
    )

    inside = [i for i in range(total) if i % depth % 2 == 1 and i % depth < depth - 1]
    second = [(i, i + 1) for i in inside] + [(i + 1, i) for i in inside]
    from_a = swap_bit(send_a, 0, total)
    from_b = lax.ppermute(send_b, "space", second)

    half_rows = cells // 2
    other_raw = [
        lax.ppermute(grad_out[k * half_rows : (k + 1) * half_rows], "chan", swap)
        for k in range(2)
    ]
    inner_a, mark, fx, fy, fz = weight_grad_inner(
        features, grad_out, mask_rows, PAIRS[:2], True
    )
    scale = 1.0 / math.sqrt(cells * total)
    if plane_side == 2:
        sx, sy = 2 * depth, depth
        zl, zh, xs, ys, es, part = edges(place, from_a, from_b, xf, yf, weights, mark)
        xh = lax.ppermute(xs, "space", [(i, i ^ sx) for i in range(total)])
        yh = lax.ppermute(ys, "space", [(i, i ^ sy) for i in range(total)])
        eh = lax.ppermute(es, "space", [(i, i ^ sx ^ sy) for i in range(total)])
        inner_b, _ = weight_grad_inner(
            features, grad_out, mask_rows, PAIRS[2:], False, es
        )
        borders = pair_borders(cx, cy, xh, yh, eh, zl, zh)
        keep, send, flat = weight_grad_rim(
            core[None], fx, fy, fz, borders, inner_a, inner_b, scale, total,
            (xh, yh, zl, zh, eh), other_raw[0],
        )
        borders = (flat,)
        other_borders = (lax.ppermute(flat, "chan", swap),)
    else:
        cube = grad_out.reshape(SPAN, SPAN, SPAN, HALF)
        mask = mask_rows.astype(BF).reshape(SPAN, SPAN, SPAN, 1)
        zl = jnp.where(even, from_b, from_a)
        zh = jnp.where(even, from_a, from_b)
        borders = wide_borders(cube * mask, zl, zh, plane_side, depth)
        inner_b, _ = weight_grad_inner(features, grad_out, mask_rows, PAIRS[2:], False)
        keep, send = weight_grad_rim(
            core[None], fx, fy, fz, borders, inner_a, inner_b, scale, total, ()
        )
        other_borders = tuple(lax.ppermute(v, "chan", swap) for v in borders)
        part = lax.dynamic_slice(weights, (place[3], place[4], 0), (TAPS, HALF, HALF))

    part = lax.ppermute(part, "chan", swap)
    part_b = swap_bit(part, 0, total)
    recv = swap_bit(send, 0, total)

    bits = total.bit_length() - 1
    rows = keep.shape[1]
    cut = rows // 2
    keep = keep.reshape((2,) * (bits - 1) + (rows, HALF))
    recv = recv.reshape(keep.shape)
    orders = [list(range(1, bits)), list(range(2, bits)) + [1]]
    have = [list(range(bits - 1, 0, -1)) for _ in orders]
    bounds = [
        (0, cut, have[0].index(orders[0][0])),
        (cut, rows, have[1].index(orders[1][0])),
    ]
    stay1, go1, stay2, go2 = split(
        keep, recv, [bit_of(index, order[0]) for order in orders], bounds
    )
    stays, gos = [stay1, stay2], [go1, go2]
    partial_out = None
    for step in range(bits - 1):
        got = [swap_bit(go, order[step], total) for go, order in zip(gos, orders)]
        ahead = ()
        if step == 0:
            partial_out, mark = data_grad_local(
                place, mask_rows, borders, (grad_out, weights), False, *gos
            )
            ahead = (mark, other_raw[1])
        if step == 1:
            data_out, mark = data_grad_local(
                place, mask_rows, other_borders,
                (*other_raw, part, part_b, partial_out), True, *gos,
            )
            ahead = (mark,)
        if step == bits - 2:
            weight_out = jnp.concatenate([s + g for s, g in zip(stays, got)], axis=0)
            break
        for k, order in enumerate(orders):
            have[k].remove(order[step])
            nxt = order[step + 1]
            stays[k], gos[k] = split(
                stays[k],
                got[k],
                [bit_of(index, nxt)],
                [(0, stays[k].shape[-2], have[k].index(nxt))],
                *ahead,
            )
    return data_out, weight_out

def solution(mesh):
    placed = (
        P("space", None),
        P("space", "chan"),
        P(None, None, "chan"),
        P("space"),
        P("space", None),
        P("space"),
    )
    return jax.shard_map(
        body,
        mesh=mesh,
        in_specs=placed,
        out_specs=(P("space", "chan"), P("space", "chan")),
        check_vma=False,
    )
```

```python
import functools
import math

import jax
import jax.numpy as jnp
from jax import lax
from jax.experimental import pallas as pl
from jax.experimental.pallas import tpu as pltpu
from jax.sharding import PartitionSpec as P

EDGE = 8
LAYERZ = 2
NBLK = 8
SPAN = 2 * EDGE
PLANE = SPAN * SPAN
HALF = 128
BF = jnp.bfloat16
F32 = jnp.float32

SHIFTS = [(a, b) for a in (-1, 0, 1) for b in (-1, 0, 1)]
PAIRS = [(0, 1), (2, 3), (4, 5), (6, 7), (8,)]


def locate_side(device_total):
    plane_side = 1
    for candidate in range(1, 33):
        if 2 * candidate**3 == device_total:
            plane_side = candidate
    return plane_side


VMEM_SPEC = pl.BlockSpec(memory_space=pltpu.VMEM)
SMEM_SPEC = pl.BlockSpec(memory_space=pltpu.SMEM)
HBM_SPEC = pl.BlockSpec(memory_space=pltpu.HBM)
ANY_SPEC = pl.BlockSpec(memory_space=pl.ANY)
TAPS = 14
COST = pl.CostEstimate(flops=1, bytes_accessed=1, transcendentals=0)
MARK = jax.ShapeDtypeStruct((8, HALF), F32)


def faces_kernel(place_ref, list_ref, count_ref, raw_ref, occ_ref, mask_ref, sa_ref, sb_ref, xf_ref, yf_ref):
    even, px, py = place_ref[0], place_ref[1], place_ref[2]
    count = count_ref[0]
    x_at = lax.broadcasted_iota(jnp.int32, (SPAN, PLANE), 0)
    q_at = lax.broadcasted_iota(jnp.int32, (SPAN, PLANE), 1)
    y_at, z_at = q_at // SPAN, q_at % SPAN
    block = (x_at // EDGE) * (2 * LAYERZ) + (y_at // EDGE) * LAYERZ + z_at // EDGE
    active = jnp.zeros((SPAN, PLANE), F32)
    for j in range(NBLK):
        live = jnp.where(j < count, 1.0, 0.0).astype(F32)
        active += jnp.where(block == list_ref[0, j], live, 0.0)
    mask_ref[...] = active * occ_ref[...].astype(F32)

    za = jnp.where(even == 1, SPAN - 1, 0)
    row = lax.broadcasted_iota(jnp.int32, (3 * SPAN, PLANE), 0)
    col = lax.broadcasted_iota(jnp.int32, (3 * SPAN, PLANE), 1)
    kind, at = row // SPAN, row % SPAN
    depth = jnp.where(kind == 0, za, SPAN - 1 - za)
    target = jnp.where(kind == 2, py * SPAN + at, at * SPAN + depth)
    chosen = (col == target).astype(F32)
    for x in range(SPAN):
        left = (chosen * mask_ref[x : x + 1, :]).astype(BF)
        got = jnp.dot(left, raw_ref[x * PLANE : (x + 1) * PLANE, :], preferred_element_type=F32)
        got = got.astype(BF)
        sa_ref[x] = got[0:SPAN]
        sb_ref[x] = got[SPAN : 2 * SPAN]
        yf_ref[x] = got[2 * SPAN :]
    row = lax.broadcasted_iota(jnp.int32, (PLANE, PLANE), 0)
    col = lax.broadcasted_iota(jnp.int32, (PLANE, PLANE), 1)
    left = ((row == col).astype(F32) * mask_ref[pl.ds(px, 1), :]).astype(BF)
    plane = raw_ref[pl.ds(pl.multiple_of(px * PLANE, PLANE), PLANE), :]
    got = jnp.dot(left, plane, preferred_element_type=F32).astype(BF)
    xf_ref[...] = got.reshape(SPAN, SPAN, HALF)


def faces(place, block_list, block_count, raw, occupancy):
    face = jax.ShapeDtypeStruct((SPAN, SPAN, HALF), BF)
    return pl.pallas_call(
        faces_kernel,
        out_shape=(jax.ShapeDtypeStruct((SPAN, PLANE), F32), face, face, face, face),
        in_specs=[SMEM_SPEC] * 3 + [VMEM_SPEC] * 2,
        out_specs=(VMEM_SPEC,) * 5,
        compiler_params=pltpu.CompilerParams(vmem_limit_bytes=12 << 20),
        cost_estimate=COST,
        name="faces",
    )(place, block_list, block_count, raw, occupancy.reshape(SPAN, PLANE))


def edges_kernel(
    place_ref, fa_ref, fb_ref, xf_ref, yf_ref, w_ref, _, zl_ref, zh_ref, xs_ref, ys_ref, es_ref, part_ref, sem
):
    even, px, py = place_ref[0], place_ref[1], place_ref[2]
    copy = pltpu.make_async_copy(
        w_ref.at[pl.ds(place_ref[3], part_ref.shape[0]), pl.ds(pl.multiple_of(place_ref[4], HALF), HALF)],
        part_ref,
        sem,
    )
    copy.start()

    @pl.when(even == 1)
    def _():
        zl_ref[...] = fb_ref[...]
        zh_ref[...] = fa_ref[...]

    @pl.when(even == 0)
    def _():
        zl_ref[...] = fa_ref[...]
        zh_ref[...] = fb_ref[...]

    xs_ref[0:SPAN] = xf_ref[...]
    ys_ref[0:SPAN] = yf_ref[...]
    es_ref[0:SPAN, :] = yf_ref[pl.ds(px, 1)].reshape(SPAN, HALF)
    row = lax.broadcasted_iota(jnp.int32, (2 * SPAN, PLANE), 0)
    col = lax.broadcasted_iota(jnp.int32, (2 * SPAN, PLANE), 1)
    total = None
    for k, ref in enumerate((zl_ref, zh_ref)):
        xs_ref[SPAN + k] = ref[pl.ds(px, 1)].reshape(SPAN, HALF)
        target = jnp.where(
            row < SPAN, row * SPAN + py, jnp.where(row == SPAN + k, px * SPAN + py, -1)
        )
        left = (col == target).astype(F32).astype(BF)
        got = jnp.dot(left, ref[...].reshape(PLANE, HALF), preferred_element_type=F32)
        ys_ref[SPAN + k] = got[0:SPAN].astype(BF)
        total = got[SPAN:] if total is None else total + got[SPAN:]
    es_ref[SPAN:, :] = total.astype(BF)
    copy.wait()


def edges(place, from_a, from_b, xf, yf, weights, mark):
    face = jax.ShapeDtypeStruct((SPAN, SPAN, HALF), BF)
    strip = jax.ShapeDtypeStruct((SPAN + 2, SPAN, HALF), BF)
    corner = jax.ShapeDtypeStruct((2 * SPAN, HALF), BF)
    return pl.pallas_call(
        edges_kernel,
        out_shape=(
            face, face, strip, strip, corner,
            jax.ShapeDtypeStruct((TAPS, HALF, HALF), BF),
        ),
        in_specs=[SMEM_SPEC] + [VMEM_SPEC] * 4 + [HBM_SPEC, ANY_SPEC],
        out_specs=(VMEM_SPEC,) * 5 + (HBM_SPEC,),
        scratch_shapes=[pltpu.SemaphoreType.DMA],
        compiler_params=pltpu.CompilerParams(vmem_limit_bytes=8 << 20),
        cost_estimate=COST,
        name="edges",
    )(place, from_a, from_b, xf, yf, weights, mark)

def keep_column(mask_ref, x):
    return jnp.broadcast_to(mask_ref[x : x + 1, :], (8, PLANE)).T[:, 0:1]


def unpack(place_ref, flat_ref, gp_ref, zp_ref):
    cx, cy = place_ref[6], place_ref[7]
    near_x, far_x = (SPAN + 1) * (1 - cx), (SPAN + 1) * cx
    near_y, far_y = (SPAN + 1) * (1 - cy), (SPAN + 1) * cy
    n = (SPAN + 2) * SPAN
    zero = jnp.zeros((SPAN, HALF), BF)

    def rows(first, count=SPAN):
        return flat_ref[first : first + count, :]

    for x in range(SPAN + 2):
        gp_ref[far_x, x] = zero
        gp_ref[x, far_y] = zero
    for y in range(SPAN):
        gp_ref[near_x, y + 1] = rows(y * SPAN)
        gp_ref[y + 1, near_y] = rows(n + y * SPAN)
    gp_ref[near_x, far_y] = zero
    gp_ref[near_x, near_y] = rows(2 * n + 2 * PLANE)
    place = lax.broadcasted_iota(jnp.int32, (SPAN, SPAN, HALF), 1)
    single = lax.broadcasted_iota(jnp.int32, (SPAN, HALF), 0)
    for side in range(2):
        face = rows(2 * n + side * PLANE, PLANE).astype(F32).reshape(SPAN, SPAN, HALF)
        strip = rows(n + (SPAN + side) * SPAN).astype(F32)
        x_row = rows((SPAN + side) * SPAN).astype(F32)
        corner = flat_ref[2 * n + 2 * PLANE + SPAN :, :].astype(F32)[side : side + 1, :]
        low, high = (jnp.where(cy == want, strip, 0.0).reshape(SPAN, 1, HALF) for want in (1, 0))
        c_low, c_high = (jnp.where(cy == want, corner, 0.0) for want in (1, 0))
        moved = [
            jnp.where(place == SPAN - 1, high, jnp.roll(face, -1, 1)),
            face,
            jnp.where(place == 0, low, jnp.roll(face, 1, 1)),
        ]
        moved_row = [
            jnp.where(single == SPAN - 1, c_high, jnp.roll(x_row, -1, 0)),
            x_row,
            jnp.where(single == 0, c_low, jnp.roll(x_row, 1, 0)),
        ]
        for b in range(3):
            zp_ref[side, b, 1 : 1 + SPAN] = moved[b].astype(BF)
            zp_ref[side, b, far_x] = zero
            zp_ref[side, b, near_x] = moved_row[b].astype(BF)


def assemble(raw_refs, mask_ref, yb_ref, gp_ref):
    each = SPAN // len(raw_refs)
    for x in range(SPAN):
        rows = slice(x % each * PLANE, (x % each + 1) * PLANE)
        block = raw_refs[x // each][rows, :].astype(F32) * keep_column(mask_ref, x)
        gp_ref[x + 1, 1 : 1 + SPAN] = block.astype(BF).reshape(SPAN, SPAN, HALF)
        if yb_ref is not None:
            gp_ref[x + 1, 0] = yb_ref[0, x]
            gp_ref[x + 1, SPAN + 1] = yb_ref[1, x]


def load_features(feat_ref, mask_ref, f_ref, rims):
    cin = feat_ref.shape[1]
    src = lax.broadcasted_iota(jnp.int32, (PLANE, 3 * PLANE), 0)
    col = lax.broadcasted_iota(jnp.int32, (PLANE, 3 * PLANE), 1)
    dst = col % PLANE
    at = dst % SPAN + col // PLANE - 1
    shift = (at >= 0) & (at < SPAN) & (src == dst // SPAN * SPAN + at)
    shift = shift.astype(F32).astype(BF)

    def spread(block, *outs):
        moved = jnp.dot(block, shift, preferred_element_type=F32).astype(BF)
        for ref, cols in outs:
            ref[0:cin, cols] = moved[:, 0:PLANE]
            ref[cin : 2 * cin, cols] = block
            ref[2 * cin :, cols] = moved[:, 2 * PLANE :]

    row = lax.broadcasted_iota(jnp.int32, (4 * SPAN, PLANE), 0)
    pos = lax.broadcasted_iota(jnp.int32, (4 * SPAN, PLANE), 1)
    kind, r = row // SPAN, row % SPAN
    target = jnp.where(kind < 2, kind * (PLANE - SPAN) + r, r * SPAN + (kind - 2) * (SPAN - 1))
    chosen = (pos == target).astype(F32)
    found = []
    whole = slice(0, PLANE)
    for x in range(SPAN):
        cols = slice(x * PLANE, (x + 1) * PLANE)
        plane = feat_ref[cols, :]
        mask = mask_ref[x : x + 1, :]
        outs = [(f_ref, cols)]
        if rims and x in (0, SPAN - 1):
            outs.append((rims[0].at[x % 2], whole))
        spread((plane.T.astype(F32) * mask).astype(BF), *outs)
        if rims:
            left = (chosen * mask).astype(BF)
            found.append(jnp.dot(left, plane, preferred_element_type=F32))
    if rims:
        for side in range(2):
            rim = [v[side * SPAN : (side + 1) * SPAN] for v in found]
            spread(jnp.concatenate(rim, axis=0).astype(BF).T, (rims[1].at[side], whole))
            rim = [v[(side + 2) * SPAN : (side + 3) * SPAN] for v in found]
            rims[2][side] = jnp.concatenate(rim, axis=0).astype(BF).T


def inner_kernel(feat_ref, raw_ref, mask_ref, *refs, pairs, ignored):
    out_ref, mark_ref, *rims, f_ref, gp_ref, hold_ref, sems = refs[ignored:]
    cin = feat_ref.shape[1]
    copies = []

    def leave(source, target):
        copy = pltpu.make_async_copy(source, target, sems.at[len(copies)])
        copy.start()
        copies.append(copy)

    if rims:
        held = rims[3:]
        load_features(feat_ref, mask_ref, f_ref, held)
    else:
        load_features(feat_ref, mask_ref, f_ref, ())
    zero = jnp.zeros((SPAN, HALF), BF)
    for y in range(SPAN + 2):
        gp_ref[0, y] = zero
        gp_ref[SPAN + 1, y] = zero
    for x in range(SPAN):
        block = raw_ref[x * PLANE : (x + 1) * PLANE, :].astype(F32) * keep_column(mask_ref, x)
        gp_ref[x + 1, 1 : 1 + SPAN] = block.astype(BF).reshape(SPAN, SPAN, HALF)
        gp_ref[x + 1, 0] = zero
        gp_ref[x + 1, SPAN + 1] = zero

    def source(shift):
        a, b = SHIFTS[shift]
        block = gp_ref[1 - a : 1 - a + SPAN, 1 - b : 1 - b + SPAN]
        return block.reshape(SPAN * PLANE, HALF)

    mark_ref[...] = jnp.zeros_like(mark_ref)
    for pair in pairs:
        right = jnp.concatenate([source(s) for s in pair], axis=1)
        acc = jnp.dot(f_ref[...], right, preferred_element_type=F32)
        for c in range(3):
            for k, s in enumerate(pair):
                tap = 3 * (s - pairs[0][0]) + c
                hold_ref[tap] = acc[c * cin : (c + 1) * cin, HALF * k : HALF * (k + 1)]
    leave(hold_ref, out_ref)
    if rims:
        for source, target in zip(held, rims[:3]):
            leave(source, target)
    for copy in copies:
        copy.wait()


def weight_grad_inner(features, raw, mask_rows, pairs, with_rims, *ahead):
    cells, cin = features.shape
    taps = 3 * sum(len(pair) for pair in pairs)
    outs = [jax.ShapeDtypeStruct((taps, cin, HALF), F32), MARK]
    held = []
    if with_rims:
        held = [(2, 3 * cin, PLANE), (2, 3 * cin, PLANE), (2, cin, PLANE)]
        outs += [jax.ShapeDtypeStruct(shape, BF) for shape in held]
    return pl.pallas_call(
        functools.partial(inner_kernel, pairs=pairs, ignored=len(ahead)),
        out_shape=tuple(outs),
        in_specs=[VMEM_SPEC] * 3 + [ANY_SPEC] * len(ahead),
        out_specs=(HBM_SPEC, VMEM_SPEC) + (HBM_SPEC,) * len(held),
        scratch_shapes=[pltpu.VMEM(shape, BF) for shape in held]
        + [
            pltpu.VMEM((3 * cin, cells), BF),
            pltpu.VMEM((SPAN + 2, SPAN + 2, SPAN, HALF), BF),
            pltpu.VMEM((taps, cin, HALF), F32),
            pltpu.SemaphoreType.DMA((len(held) + 1,)),
        ],
        compiler_params=pltpu.CompilerParams(vmem_limit_bytes=28 << 20),
        cost_estimate=pl.CostEstimate(
            flops=0 if with_rims else 1 << 31, bytes_accessed=1, transcendentals=0
        ),
        name="weight_inner",
    )(features, raw, mask_rows, *ahead)


def rim_kernel(
    mine_ref, fx_ref, fy_ref, fz_ref, xb_ref, yb_ref, zp_ref, part_a_ref, part_b_ref,
    *refs, scale, pieces, ignored
):
    parts, refs = refs[:pieces], refs[pieces + ignored :]
    keep_ref, send_ref, *flat_refs, acc_ref, sems = refs
    at = 0
    for ref in parts:
        for block in range(ref.shape[0] if len(ref.shape) == 3 else 1):
            value = ref[block] if len(ref.shape) == 3 else ref[...]
            flat_refs[0][at : at + value.shape[0], :] = value
            at += value.shape[0]
    cin = fz_ref.shape[1]
    rows = acc_ref.shape[-2]
    bits = len(acc_ref.shape) - 2
    zero = jnp.zeros((1, SPAN, HALF), BF)
    more = {}

    def add(shift, c, value):
        more.setdefault(3 * shift + c, []).append(value)

    for side in range(2):
        first = 6 if side == 0 else 0
        right = jnp.concatenate(
            [xb_ref[side, 1 - b : 1 - b + SPAN].reshape(PLANE, HALF) for b in (-1, 0, 1)], axis=1
        )
        got = jnp.dot(fx_ref[side], right, preferred_element_type=F32)
        for b in range(3):
            for c in range(3):
                add(first + b, c, got[c * cin : (c + 1) * cin, b * HALF : (b + 1) * HALF])
        strip = jnp.concatenate([zero, yb_ref[side], zero], axis=0)
        right = jnp.concatenate(
            [strip[1 - a : 1 - a + SPAN].reshape(PLANE, HALF) for a in (-1, 0, 1)], axis=1
        )
        got = jnp.dot(fy_ref[side], right, preferred_element_type=F32)
        for a in range(3):
            for c in range(3):
                shift = 3 * a + (2 if side == 0 else 0)
                add(shift, c, got[c * cin : (c + 1) * cin, a * HALF : (a + 1) * HALF])
        for pair in PAIRS:
            cols = []
            for s in pair:
                a, b = SHIFTS[s]
                cols.append(zp_ref[side, b + 1, 1 - a : 1 - a + SPAN].reshape(PLANE, HALF))
            got = jnp.dot(
                fz_ref[side], jnp.concatenate(cols, axis=1), preferred_element_type=F32
            )
            for k, s in enumerate(pair):
                add(s, 2 if side == 0 else 0, got[:, k * HALF : (k + 1) * HALF])

    for tap in range(27):
        taps_a = part_a_ref.shape[0]
        value = part_a_ref[tap] if tap < taps_a else part_b_ref[tap - taps_a]
        for extra in more.get(tap, []):
            value = value + extra
        value = value * scale
        first = tap * cin
        while first < (tap + 1) * cin:
            block, at = divmod(first, rows)
            count = min(rows - at, (tap + 1) * cin - first)
            piece = value[first - tap * cin : first - tap * cin + count]
            spot = (block % 2,) + tuple(block // 2 ** (bits - 1 - k) % 2 for k in range(bits - 1))
            acc_ref[spot + (slice(at, at + count),)] = piece
            first += count

    mine = mine_ref[0]
    out_send = pltpu.make_async_copy(acc_ref.at[1 - mine], send_ref, sems.at[0])
    out_keep = pltpu.make_async_copy(acc_ref.at[mine], keep_ref, sems.at[1])
    out_send.start()
    out_keep.start()
    out_send.wait()
    out_keep.wait()


def weight_grad_rim(mine, fx, fy, fz, borders, inner_a, inner_b, scale, total, pieces, *ahead):
    cin = fz.shape[1]
    rows = 27 * cin // total
    by_bit = (2,) * (total.bit_length() - 2)
    outs = [jax.ShapeDtypeStruct(by_bit + (rows, HALF), F32)] * 2
    if pieces:
        length = sum(v.size for v in pieces) // HALF
        outs.append(jax.ShapeDtypeStruct((length, HALF), BF))
    return pl.pallas_call(
        functools.partial(rim_kernel, scale=scale, pieces=len(pieces), ignored=len(ahead)),
        out_shape=tuple(outs),
        in_specs=[SMEM_SPEC] + [VMEM_SPEC] * (8 + len(pieces)) + [ANY_SPEC] * len(ahead),
        out_specs=(ANY_SPEC, ANY_SPEC) + (VMEM_SPEC,) * (len(outs) - 2),
        scratch_shapes=[
            pltpu.VMEM((2,) + by_bit + (rows, HALF), F32),
            pltpu.SemaphoreType.DMA((2,)),
        ],
        compiler_params=pltpu.CompilerParams(vmem_limit_bytes=24 << 20),
        cost_estimate=COST,
        name="weight_rim",
    )(mine, fx, fy, fz, *borders, inner_a, inner_b, *pieces, *ahead)


def data_kernel(place_ref, mask_ref, *refs, borders, ignored, last):
    around, refs = refs[:borders], refs[borders:]
    *refs, z_ref = refs
    if last:
        *raw_refs, wa_ref, wb_ref, prev_ref = refs[:5]
        out_ref, mark_ref, gp_ref, wt_ref, h_ref = refs[5 + ignored :]
        first_core = place_ref[0] == 1

        def tile_of(tap):
            low = min(tap, TAPS - 1)
            high = max(tap - (27 - TAPS), 0)
            if tap < 27 - TAPS:
                return jnp.where(first_core, wa_ref[low], wb_ref[low])
            if tap >= TAPS:
                return jnp.where(first_core, wb_ref[high], wa_ref[high])
            return jnp.where(first_core, wa_ref[low], wa_ref[high])
    else:
        raw_ref, whole_ref = refs[:2]
        out_ref, mark_ref, gp_ref, wt_ref, h_ref, w_ref, sem = refs[2 + ignored :]
        raw_refs, prev_ref = [raw_ref], None
        copy = pltpu.make_async_copy(whole_ref.at[:, pl.ds(pl.multiple_of(place_ref[5], HALF), HALF)], w_ref, sem)
        copy.start()

        def tile_of(tap):
            return w_ref[tap]

    mark_ref[...] = jnp.zeros_like(mark_ref)
    if borders == 1:
        zp_ref = z_ref
        unpack(place_ref, around[0], gp_ref, zp_ref)
        assemble(raw_refs, mask_ref, None, gp_ref)
    else:
        xb_ref, yb_ref, zp_ref = around
        gp_ref[0] = xb_ref[0]
        gp_ref[SPAN + 1] = xb_ref[1]
        assemble(raw_refs, mask_ref, yb_ref, gp_ref)
    if not last:
        copy.wait()
    for s in range(9):
        for c in range(3):
            tile = tile_of(3 * s + c).astype(F32).T.astype(BF)
            wt_ref[s * HALF : (s + 1) * HALF, c * HALF : (c + 1) * HALF] = tile

    for side, c in ((0, 2), (1, 0)):
        cols = []
        for s in range(9):
            a, b = SHIFTS[s]
            cols.append(zp_ref[side, b + 1, 1 - a : 1 - a + SPAN].reshape(PLANE, HALF))
        h_ref[side] = jnp.dot(
            jnp.concatenate(cols, axis=1),
            wt_ref[:, c * HALF : (c + 1) * HALF],
            preferred_element_type=F32,
        ).reshape(SPAN, SPAN, HALF)

    zpos = lax.broadcasted_iota(jnp.int32, (SPAN, SPAN, HALF), 1)

    def plane(x, _):
        cols = []
        for s in range(9):
            a, b = SHIFTS[s]
            block = gp_ref[pl.ds(x + 1 - a, 1), 1 - b : 1 - b + SPAN]
            cols.append(block.reshape(PLANE, HALF))
        prod = jnp.dot(jnp.concatenate(cols, axis=1), wt_ref[...], preferred_element_type=F32)
        down = pltpu.roll(prod[:, 0:HALF], PLANE - 1, 0).reshape(SPAN, SPAN, HALF)
        mid = prod[:, HALF : 2 * HALF].reshape(SPAN, SPAN, HALF)
        up = pltpu.roll(prod[:, 2 * HALF :], 1, 0).reshape(SPAN, SPAN, HALF)
        low = h_ref[0, pl.ds(x, 1)].reshape(SPAN, 1, HALF)
        high = h_ref[1, pl.ds(x, 1)].reshape(SPAN, 1, HALF)
        full = mid + jnp.where(zpos == 0, low, up) + jnp.where(zpos == SPAN - 1, high, down)
        full = full.reshape(PLANE, HALF)
        rows = pl.ds(pl.multiple_of(x * PLANE, PLANE), PLANE)
        if prev_ref is None:
            out_ref[rows, :] = full
        else:
            keep = jnp.broadcast_to(mask_ref[pl.ds(x, 1), :], (8, PLANE)).T[:, 0:1]
            out_ref[rows, :] = ((full + prev_ref[rows, :]) * keep).astype(BF)
        return 0

    lax.fori_loop(0, SPAN, plane, 0, unroll=4)


def data_grad_local(place, mask_rows, borders, operands, last, *ahead):
    scratch = [
        pltpu.VMEM((SPAN + 2, SPAN + 2, SPAN, HALF), BF),
        pltpu.VMEM((9 * HALF, 3 * HALF), BF),
        pltpu.VMEM((2, SPAN, SPAN, HALF), F32),
    ]
    specs = [VMEM_SPEC] * len(operands)
    if not last:
        specs[-1] = HBM_SPEC
        scratch += [pltpu.VMEM((27, HALF, HALF), BF), pltpu.SemaphoreType.DMA]
    scratch.append(pltpu.VMEM((2, 3, SPAN + 2, SPAN, HALF), BF))
    return pl.pallas_call(
        functools.partial(
            data_kernel, borders=len(borders), ignored=len(ahead), last=last
        ),
        out_shape=(
            jax.ShapeDtypeStruct((SPAN * PLANE, HALF), BF if last else F32),
            MARK,
        ),
        in_specs=[SMEM_SPEC] + [VMEM_SPEC] * (1 + len(borders)) + specs + [ANY_SPEC] * len(ahead),
        out_specs=(VMEM_SPEC, VMEM_SPEC),
        scratch_shapes=scratch,
        compiler_params=pltpu.CompilerParams(vmem_limit_bytes=20 << 20),
        cost_estimate=COST,
        name="data_grad",
    )(place, mask_rows, *borders, *operands, *ahead)


def split_kernel(bits_ref, keep_ref, recv_ref, *outs, bounds, ignored):
    outs = outs[ignored:]
    for k, (low, high, lead) in enumerate(bounds):
        stay_ref, go_ref = outs[2 * k], outs[2 * k + 1]
        shape = keep_ref.shape
        mine = bits_ref[k]
        before = math.prod(shape[:lead])
        for ref, bit in ((stay_ref, mine), (go_ref, 1 - mine)):
            for i in range(before):
                at = []
                for size in reversed(shape[:lead]):
                    i, rest = divmod(i, size)
                    at.insert(0, rest)
                at = tuple(at)
                tail = (slice(None),) * (len(shape) - 3 - lead)
                src = at + (bit,) + tail + (slice(low, high),)
                ref[at] = keep_ref[src] + recv_ref[src]


def split(keep, recv, bits, bounds, *ahead):
    outs = []
    for low, high, lead in bounds:
        shape = keep.shape[:lead] + keep.shape[lead + 1 : -2] + (high - low, HALF)
        outs += [jax.ShapeDtypeStruct(shape, F32)] * 2
    return pl.pallas_call(
        functools.partial(split_kernel, bounds=bounds, ignored=len(ahead)),
        out_shape=tuple(outs),
        in_specs=[SMEM_SPEC, VMEM_SPEC, VMEM_SPEC] + [ANY_SPEC] * len(ahead),
        out_specs=tuple(VMEM_SPEC for _ in outs),
        compiler_params=pltpu.CompilerParams(vmem_limit_bytes=12 << 20),
        cost_estimate=COST,
        name="add_split",
    )(jnp.stack(bits), keep, recv, *ahead)


def swap_bit(block, bit, total):
    return lax.ppermute(block, "space", [(i, i ^ (1 << bit)) for i in range(total)])


def bit_of(index, bit):
    return (index // (1 << bit) % 2).astype(jnp.int32)


def extend(block, dim, stride, coords, side):
    total = lax.axis_size("space")
    length = block.shape[dim]
    first = lax.slice_in_dim(block, 0, 1, axis=dim)
    last = lax.slice_in_dim(block, length - 1, length, axis=dim)
    below = lax.ppermute(
        last, "space", [(i, i + stride) for i in range(total) if coords(i) < side - 1]
    )
    above = lax.ppermute(
        first, "space", [(i + stride, i) for i in range(total) if coords(i) < side - 1]
    )
    return jnp.concatenate([below, block, above], axis=dim)


def turned(face):
    return jnp.stack([face[:, 1 - b : 1 - b + SPAN] for b in (-1, 0, 1)])


def wide_borders(masked, zl, zh, plane_side, depth):
    block = jnp.concatenate([zl[:, :, None], masked, zh[:, :, None]], axis=2)
    block = extend(block, 1, depth, lambda i: i // depth % plane_side, plane_side)
    block = extend(block, 0, depth * plane_side, lambda i: i // (depth * plane_side), plane_side)
    inner = block[:, :, 1 : 1 + SPAN]
    xb = jnp.stack([inner[0], inner[SPAN + 1]])
    yb = jnp.stack([inner[1 : 1 + SPAN, 0], inner[1 : 1 + SPAN, SPAN + 1]])
    zp = jnp.stack([turned(block[:, :, 0]), turned(block[:, :, SPAN + 1])])
    return xb, yb, zp


def pair_borders(cx, cy, xh, yh, eh, zl, zh):
    def both(value, coord, axis):
        zero = jnp.zeros_like(value)
        low = jnp.where(coord == 1, value, zero)
        high = jnp.where(coord == 0, value, zero)
        return jnp.expand_dims(low, axis), jnp.expand_dims(high, axis)

    def around(values, corner, axis):
        low, high = both(corner, cy, axis)
        return jnp.concatenate([low, values, high], axis=axis)

    xb = jnp.concatenate(both(around(xh[:SPAN], eh[:SPAN], 0), cx, 0))
    yb = jnp.concatenate(both(yh[:SPAN], cy, 0))

    def face(z, k):
        rows = around(z, yh[k], 1)
        low, high = both(around(xh[k], eh[k], 0), cx, 0)
        return turned(jnp.concatenate([low, rows, high], axis=0))

    zp = jnp.stack([face(zl, SPAN), face(zh, SPAN + 1)])
    return xb, yb, zp


def body(features, grad_out, weights, occupancy, block_list, block_count):
    total = lax.axis_size("space")
    plane_side = locate_side(total)
    depth = 2 * plane_side
    cells, cin = features.shape
    index = lax.axis_index("space")
    column = lax.axis_index("chan")
    swap = [(0, 1), (1, 0)]
    cx = index // (plane_side * depth)
    cy = index // depth % plane_side
    even = index % 2 == 0

    core = bit_of(index, 0)
    place = jnp.stack(
        [
            (index + 1) % 2,
            jnp.where(cx == 0, SPAN - 1, 0),
            jnp.where(cy == 0, SPAN - 1, 0),
            core * (27 - TAPS),
            (1 - column) * HALF,
            column * HALF,
            cx,
            cy,
        ]
    ).astype(jnp.int32)
    mask_rows, send_a, send_b, xf, yf = faces(
        place, block_list, block_count, grad_out, occupancy
    )

    inside = [i for i in range(total) if i % depth % 2 == 1 and i % depth < depth - 1]
    second = [(i, i + 1) for i in inside] + [(i + 1, i) for i in inside]
    from_a = swap_bit(send_a, 0, total)
    from_b = lax.ppermute(send_b, "space", second)

    half_rows = cells // 2
    other_raw = [
        lax.ppermute(grad_out[k * half_rows : (k + 1) * half_rows], "chan", swap)
        for k in range(2)
    ]
    inner_a, mark, fx, fy, fz = weight_grad_inner(
        features, grad_out, mask_rows, PAIRS[:2], True
    )
    scale = 1.0 / math.sqrt(cells * total)
    if plane_side == 2:
        sx, sy = 2 * depth, depth
        zl, zh, xs, ys, es, part = edges(place, from_a, from_b, xf, yf, weights, mark)
        xh = lax.ppermute(xs, "space", [(i, i ^ sx) for i in range(total)])
        yh = lax.ppermute(ys, "space", [(i, i ^ sy) for i in range(total)])
        eh = lax.ppermute(es, "space", [(i, i ^ sx ^ sy) for i in range(total)])
        inner_b, _ = weight_grad_inner(
            features, grad_out, mask_rows, PAIRS[2:], False, xs, ys, es
        )
        borders = pair_borders(cx, cy, xh, yh, eh, zl, zh)
        keep, send, flat = weight_grad_rim(
            core[None], fx, fy, fz, borders, inner_a, inner_b, scale, total,
            (xh, yh, zl, zh, eh), other_raw[0],
        )
        borders = (flat,)
        other_borders = (lax.ppermute(flat, "chan", swap),)
    else:
        cube = grad_out.reshape(SPAN, SPAN, SPAN, HALF)
        mask = mask_rows.astype(BF).reshape(SPAN, SPAN, SPAN, 1)
        zl = jnp.where(even, from_b, from_a)
        zh = jnp.where(even, from_a, from_b)
        borders = wide_borders(cube * mask, zl, zh, plane_side, depth)
        inner_b, _ = weight_grad_inner(features, grad_out, mask_rows, PAIRS[2:], False)
        keep, send = weight_grad_rim(
            core[None], fx, fy, fz, borders, inner_a, inner_b, scale, total, ()
        )
        other_borders = tuple(lax.ppermute(v, "chan", swap) for v in borders)
        part = lax.dynamic_slice(weights, (place[3], place[4], 0), (TAPS, HALF, HALF))

    part = lax.ppermute(part, "chan", swap)
    part_b = swap_bit(part, 0, total)
    recv = swap_bit(send, 0, total)

    bits = total.bit_length() - 1
    rows = keep.shape[-2]
    cut = rows // 2
    orders = [list(range(1, bits)), list(range(2, bits)) + [1]]
    have = [list(range(bits - 1, 0, -1)) for _ in orders]
    bounds = [
        (0, cut, have[0].index(orders[0][0])),
        (cut, rows, have[1].index(orders[1][0])),
    ]
    stay1, go1, stay2, go2 = split(
        keep, recv, [bit_of(index, order[0]) for order in orders], bounds
    )
    stays, gos = [stay1, stay2], [go1, go2]
    partial_out = None
    for step in range(bits - 1):
        got = [swap_bit(go, order[step], total) for go, order in zip(gos, orders)]
        ahead = ()
        if step == 0:
            partial_out, mark = data_grad_local(
                place, mask_rows, borders, (grad_out, weights), False, *gos
            )
            ahead = (mark, other_raw[1])
        if step == 1:
            data_out, mark = data_grad_local(
                place, mask_rows, other_borders,
                (*other_raw, part, part_b, partial_out), True, *gos,
            )
            ahead = (mark,)
        if step == bits - 2:
            weight_out = jnp.concatenate([s + g for s, g in zip(stays, got)], axis=0)
            break
        for k, order in enumerate(orders):
            have[k].remove(order[step])
            nxt = order[step + 1]
            stays[k], gos[k] = split(
                stays[k],
                got[k],
                [bit_of(index, nxt)],
                [(0, stays[k].shape[-2], have[k].index(nxt))],
                *ahead,
            )
    return data_out, weight_out

def solution(mesh):
    placed = (
        P("space", None),
        P("space", "chan"),
        P(None, None, "chan"),
        P("space"),
        P("space", None),
        P("space"),
    )
    return jax.shard_map(
        body,
        mesh=mesh,
        in_specs=placed,
        out_specs=(P("space", "chan"), P("space", "chan")),
        check_vma=False,
    )
```
